32 devices in a mesh: space: 4 (over y, core), energy: 8 (over z, x).
Axes of the slice: x: 2, y: 2, z: 4, core: 2. Of those that a mesh axis runs over, the one named last changes fastest.
Arguments:
- ham_diag: float32 [8, 2, 128, 128], P('space'), may hold values from -0.5 to 0.5
- coupling: float32 [8, 2, 128, 128], P('space'), may hold values from -0.5 to 0.5
- contact_left: float32 [2, 128, 128], replicated, may hold values from -0.5 to 0.5
- mode_weight: float32 [4], replicated, may hold values from 0.5 to 2
- mode_offset: int32 [4], replicated, may hold values from -4 to 4, as said below
- pattern: int32 [128, 128], replicated, may hold values 0 or 1
Outputs:
- sigma: float32 [8, 8, 2, 128, 128], P('energy', 'space')
The draws below stay inside these ranges and needn't reach their ends.
Inputs may be any that keep to these rules, and one draw needn't show every extreme that they name: `mode_offset`: the offsets are -1, 1, -4 and 4 in some order.
All inputs are finite; a program needn't handle non-finite values.
Results may differ from the reference program's by a relative error of at most 0.0003.
Values sent between devices are 32-bit elements; how exact they have to be, the bound alone decides.
No kernel may reach another device: no remote copies, remote signals or barrier semaphores. Data moves between devices by JAX's collectives and lax.ppermute only.
A program may use at most 64 MiB of HBM per device.

```python
import math
import jax
import jax.numpy as jnp
from jax import lax

B = 128
MODES = 4
NB = 8
ENERGIES = 8


def draw_mode_offset(key, part):
    half_grid = ENERGIES // 2
    offsets = jnp.array([-1, 1, 0 - half_grid, half_grid], dtype=jnp.int32)
    order = jax.random.permutation(jax.random.fold_in(key, 7), MODES)
    return offsets[order].astype(jnp.int32)


def with_ends(values, key, least, top_value):
    extent = values.shape
    spot = [jax.random.randint(jax.random.fold_in(key, axis), (), 0, extent[axis]) for axis in range(len(extent))]
    values = values.at[tuple(spot)].set(least)
    longest = extent.index(max(extent))
    spot[longest] = (spot[longest] + 1) % extent[longest]
    return values.at[tuple(spot)].set(top_value)


def levels(rng, extent, split, low, high):
    def one(position, shards_of):
        heights = jax.random.uniform(jax.random.fold_in(jax.random.fold_in(rng, 6), position), (shards_of,), jnp.float32, low / len(split), high / len(split))
        return jnp.repeat(jnp.exp(heights), extent[position] // shards_of).reshape((-1,) + (1,) * (len(extent) - position - 1))

    level = one(*split[0])
    for cut in split[1:]:
        level = level * one(*cut)
    return level


def bell_draw(own_key, dims, spread, most, cuts=(), held_as=jnp.bfloat16):
    result = spread * jax.random.normal(own_key, dims, jnp.float32)
    if cuts:
        result = result * levels(own_key, dims, cuts, -0.22, 0.18)
    return jnp.clip(result, -most, most).astype(held_as)


def setup_inputs(seed: int = 0) -> dict:
    key_list = jax.random.split(jax.random.key(seed), 7)
    ham_diag = bell_draw(key_list[0], (NB, 2, B, B), B ** -0.5, 0.5, ((0, 4),), jnp.float32)
    coupling = bell_draw(key_list[1], (NB, 2, B, B), B ** -0.5, 0.5, ((0, 4),), jnp.float32)
    contact_left = bell_draw(key_list[2], (2, B, B), B ** -0.5, 0.5, (), jnp.float32)
    mode_weight = jnp.clip(jnp.exp(jax.random.uniform(key_list[3], (MODES,), jnp.float32, math.log(0.5), math.log(2.0))), 0.5, 2.0)
    mode_offset = draw_mode_offset(jax.random.fold_in(key_list[6], 71), 0)
    pattern = with_ends((jax.random.randint(key_list[5], (B, B), 0, 2) < 1).astype(jnp.int32), jax.random.fold_in(key_list[5], 1), 0, 1)
    return {"ham_diag": ham_diag, "coupling": coupling, "contact_left": contact_left, "mode_weight": mode_weight, "mode_offset": mode_offset, "pattern": pattern}


HIGHEST = lax.Precision.HIGHEST
BROADENING = 0.1

def product(former, latter):
    real_part = jnp.dot(former[0], latter[0], precision=HIGHEST) - jnp.dot(former[1], latter[1], precision=HIGHEST)
    imag_part = jnp.dot(former[0], latter[1], precision=HIGHEST) + jnp.dot(former[1], latter[0], precision=HIGHEST)
    return jnp.stack([real_part, imag_part])

def adjoint(matrix):
    return jnp.stack([matrix[0].T, -matrix[1].T])

def times_imag(matrix):
    return jnp.stack([-matrix[1], matrix[0]])

def hermitian(matrix):
    return 0.5 * (matrix + adjoint(matrix))

def unit_block(order_size):
    identity_real = jnp.eye(order_size, dtype=jnp.float32)
    return jnp.stack([identity_real, jnp.zeros_like(identity_real)])

def invert(matrix):
    order_size = matrix.shape[1]
    real_form = jnp.concatenate([jnp.concatenate([matrix[0], -matrix[1]], 1), jnp.concatenate([matrix[1], matrix[0]], 1)], 0)
    inverse_form = jnp.linalg.inv(real_form)
    return jnp.stack([inverse_form[:order_size, :order_size], inverse_form[order_size:, :order_size]])

def green_diagonal(blocks, links):

    def forward_step(previous, element):
        diag_block, bridge = element
        sigma_link = product(adjoint(bridge), product(previous, bridge))
        return (invert(diag_block - sigma_link), sigma_link)
    sigma_before = lax.scan(forward_step, invert(blocks[0]), (blocks[1:], links))[1]

    def backward_step(following, element):
        diag_block, bridge = element
        sigma_link = product(bridge, product(following, adjoint(bridge)))
        return (invert(diag_block - sigma_link), sigma_link)
    sigma_after = lax.scan(backward_step, invert(blocks[-1]), (blocks[:-1], links), reverse=True)[1]
    padding = jnp.zeros_like(blocks[:1])
    sigma_before = jnp.concatenate([padding, sigma_before], 0)
    sigma_after = jnp.concatenate([sigma_after, padding], 0)
    return jax.vmap(invert)(blocks - sigma_before - sigma_after)

def mode_table(targets, sources, mode_weight, mode_offset):
    hits = (sources[None, :, None] == targets[:, None, None] - mode_offset[None, None, :]).astype(jnp.float32)
    return jnp.sum(hits * mode_weight[None, None, :], axis=2)

def reference(ham_diag, coupling, contact_left, mode_weight, mode_offset, pattern):
    order_size = ham_diag.shape[-1]
    unit = unit_block(order_size)
    onsite = -jax.vmap(hermitian)(ham_diag)
    onsite = onsite.at[0].add(times_imag(0.5 * product(contact_left, adjoint(contact_left))))
    onsite = onsite.at[-1].add(times_imag(0.5 * product(adjoint(coupling[-1]), coupling[-1])))
    links = coupling[:-1]
    energy_grid = jnp.arange(ENERGIES, dtype=jnp.int32)
    energies = -2.0 + 4.0 * (energy_grid.astype(jnp.float32) + 0.5) / ENERGIES

    def solve_energy(energy):
        shift = energy * unit + BROADENING * times_imag(unit)
        return green_diagonal(onsite + shift[None], links)
    green = lax.map(solve_energy, energies)
    table = mode_table(energy_grid, energy_grid, mode_weight, mode_offset)
    sigma = jnp.einsum('ef,fkxab->ekxab', table, green, precision=HIGHEST)
    return sigma * pattern.astype(jnp.float32)
```

```python
import functools

import jax
import jax.numpy as jnp
from jax import lax
from jax.experimental import pallas as pl
from jax.experimental.pallas import tpu as pltpu
from jax.sharding import PartitionSpec as P

HIGHEST = lax.Precision.HIGHEST
BROADENING = 0.1
F32 = jnp.float32
BF16 = jnp.bfloat16


FULL_STEPS = 3
SPLIT_STEPS = 6
LOW_STEPS = 3
RESIDUE_LIMIT = 1e-3
SAFE_STEPS = 64


def dot(a, b):
    return jnp.dot(a, b, preferred_element_type=F32)


def operand(b):
    n = b.shape[1] // 2
    return jnp.concatenate([b, jnp.concatenate([-b[:, n:], b[:, :n]], 1)], 0)


def halves(a):
    high = a.astype(BF16)
    return high, (a - high.astype(F32)).astype(BF16)


def mul_full(a, b):
    return jnp.dot(a, operand(b), precision=HIGHEST, preferred_element_type=F32)


def mul_split(a, b):
    a_high, a_low = halves(a)
    b_high, b_low = halves(b)
    b_high, b_low = operand(b_high), operand(b_low)
    return dot(a_high, b_high) + (dot(a_high, b_low) + dot(a_low, b_high))


def mul_low(a, b):
    return dot(a.astype(BF16), operand(b.astype(BF16)))


mul = mul_full


def adj(a):
    n = a.shape[1] // 2
    return jnp.concatenate([a[:, :n].T, -a[:, n:].T], 1)


def unit(n):
    row = lax.broadcasted_iota(jnp.int32, (n, 2 * n), 0)
    col = lax.broadcasted_iota(jnp.int32, (n, 2 * n), 1)
    return (row == col).astype(F32)


def times_half_imag(a):
    n = a.shape[1] // 2
    return jnp.concatenate([-0.5 * a[:, n:], 0.5 * a[:, :n]], 1)


def total(a):
    return jnp.sum(jnp.sum(a, axis=0, keepdims=True), axis=1, keepdims=True)


def start(a):
    back = adj(a)
    normal = mul_full(a, back)
    scale = 1.0 / jnp.sqrt(total(normal * normal))
    return back, normal, scale


def invert_fast(mats):
    n = mats[0].shape[0]
    one = unit(n)
    state = []
    for a in mats:
        back, normal, scale = start(a)
        state.append((back * scale, one - normal * scale, (0.99 * BROADENING**2) * scale))

    def step(multiply, _, state):
        fresh = []
        for x, rest, least in state:
            c = 2.0 / (1.0 + least)
            centred = (1.0 - c) * one + c * rest
            both = multiply(jnp.concatenate([x, centred], 0), centred)
            fresh.append((c * (x + both[:n]), both[n:], jnp.minimum(c * c * least, 1.0)))
        return tuple(fresh)

    state = tuple(state)
    for multiply, count in ((mul_full, FULL_STEPS), (mul_split, SPLIT_STEPS), (mul_low, LOW_STEPS)):
        state = lax.fori_loop(0, count, functools.partial(step, multiply), state)
    found, worst = [], jnp.zeros((1, 1), F32)
    for a, (x, _, _) in zip(mats, state):
        residue = one - mul_full(a, x)
        worst = worst + total(residue * residue)
        found.append(x + mul_split(x, residue))
    return found, worst


def invert_safe(mats):
    n = mats[0].shape[0]
    one = unit(n)
    found = []
    for a in mats:
        back, _, scale = start(a)

        def step(_, x):
            return x + mul_full(x, one - mul_full(a, x))

        x = lax.fori_loop(0, SAFE_STEPS, step, back * scale)
        found.append(x)
    return found, jnp.zeros((1, 1), F32)


def row_form(ref, index=None):
    if index is None:
        return jnp.concatenate([ref[0], ref[1]], 1)
    return jnp.concatenate([ref[index, 0], ref[index, 1]], 1)


def place():
    position = lax.axis_index("space")
    chip = position // 2
    core = position % 2
    right = (chip >= lax.axis_size("space") // 4).astype(jnp.int32)
    outer = (core == right).astype(jnp.int32)
    return position, core, right, outer


def prepare_kernel(ham_own, ham_far, cpl_own, cpl_far, cpl_before, contact, blocks_ref, links_ref, ends_ref, head_ref):
    _, core, right, outer = place()
    n = contact.shape[-1]
    energy_count = lax.axis_size("energy")
    rank = lax.axis_index("energy")
    half = energy_count // 2
    near = rank + 1 - 2 * (rank % 2)
    solved = jnp.where(core == 0, near, (rank + half) % energy_count)
    energy = -2.0 + (solved.astype(F32) + 0.5) * (4.0 / energy_count)
    one = unit(n)
    shift = energy * one + BROADENING * jnp.concatenate([one[:, n:], one[:, :n]], 1)
    mirrored = right == 1

    def chip_pick(own, far, low_half, index):
        mine = (core == 0) if low_half else (core == 1)
        return jnp.where(mine, row_form(own, index), row_form(far, index))

    for k in range(4):
        inner_index = jnp.where(mirrored, 1 - k % 2, k % 2)
        mine = (outer == 1) if k < 2 else (outer == 0)
        ham = jnp.where(mine, row_form(ham_own, inner_index), row_form(ham_far, inner_index))
        blocks_ref[k] = shift - 0.5 * (ham + adj(ham))
    chip_links = [chip_pick(cpl_own, cpl_far, k < 2, k % 2) for k in range(4)]
    for k in range(3):
        ahead = jnp.where(mirrored, chip_links[2 - k], chip_links[k])
        back = adj(ahead)
        links_ref[k] = jnp.where(mirrored, back, ahead)
        links_ref[3 + k] = jnp.where(mirrored, ahead, back)
    last = chip_links[3]
    before = row_form(cpl_before)
    last_back = adj(last)
    before_back = adj(before)
    lead = jnp.where(mirrored, last_back, row_form(contact))
    head_ref[...] = times_half_imag(mul(lead, adj(lead)))
    ends_ref[0] = jnp.where(mirrored, last, before_back)
    ends_ref[1] = jnp.where(mirrored, before_back, last)


B0, B1, B2, T0, P1, P2, Q, R, RECORD = range(9)


def eliminate(blocks, links, head, record, schur_ref, corner_ref, invert):
    c0, c1, c2, c0h, c1h, c2h = links
    (b0, b2), bad = invert([blocks[0] + head, blocks[2]])
    t0 = mul(b0, c0)
    p1 = mul(b2, c1h)
    p2 = mul(b2, c2)
    record[B0], record[B2], record[T0], record[P1], record[P2] = b0, b2, t0, p1, p2
    middle = blocks[1] - mul(c0h, t0) - mul(c1, p1)
    upper = mul(c1, p2)
    lower = mul(c2h, p1)
    tail = blocks[3] - mul(c2h, p2)
    (b1,), more = invert([middle])
    bad = bad + more
    q = mul(b1, upper)
    r = mul(lower, b1)
    schur = tail - mul(lower, q)
    record[B1], record[Q], record[R] = b1, q, r
    schur_ref[...] = schur
    (corner,), more = invert([schur])
    corner_ref[...] = corner
    return bad + more


def head_kernel(links_ref, message_ref, out_ref):
    link = links_ref[...]
    out_ref[...] = -mul(mul(link, message_ref[...]), adj(link))


def eliminate_kernel(blocks_ref, links_ref, head_ref, record_ref, schur_ref, corner_ref):
    def run(invert):
        return eliminate(
            [blocks_ref[k] for k in range(4)],
            [links_ref[k] for k in range(6)],
            head_ref[...],
            record_ref,
            schur_ref,
            corner_ref,
            invert,
        )

    bad = jnp.sum(run(invert_fast))

    @pl.when(jnp.logical_not(bad < RESIDUE_LIMIT))
    def _():
        run(invert_safe)


def spread_kernel(links_ref, record_ref, out_ref):
    c0, c1, c2, c0h, c1h, c2h = (links_ref[k] for k in range(6))
    b0, b1, b2, t0, p1, p2, q, r = (record_ref[k] for k in range(RECORD))
    w0 = mul(c0h, b0)
    m1 = mul(c1, b2)
    m2 = mul(c2h, b2)
    out_ref[0] = b0 + mul(mul(t0, b1), w0)
    out_ref[1] = b1
    out_ref[2] = b2 + mul(mul(p1, b1), m1)
    out_ref[3] = mul(t0, q)
    out_ref[4] = q
    out_ref[5] = mul(p1, q) + p2
    out_ref[6] = mul(r, w0)
    out_ref[7] = r
    out_ref[8] = mul(r, m1) + m2


def finish_kernel(schur_ref, spread_ref, ends_ref, message_ref, mine_ref, theirs_ref):
    _, core, right, outer = place()
    n = schur_ref.shape[0]

    def run(invert):
        link = ends_ref[1]
        closed = schur_ref[...] - mul(mul(link, message_ref[...]), adj(link))
        (full,), bad = invert([closed])
        green = [spread_ref[j] + mul(mul(spread_ref[3 + j], full), spread_ref[6 + j]) for j in range(3)] + [full]

        def store(outer_ref, inner_ref):
            for k in range(4):
                ref = outer_ref if k < 2 else inner_ref
                index = jnp.where(right == 1, 1 - k % 2, k % 2)
                ref[index, 0] = green[k][:, :n]
                ref[index, 1] = green[k][:, n:]

        @pl.when(outer == 1)
        def _():
            store(mine_ref, theirs_ref)

        @pl.when(outer == 0)
        def _():
            store(theirs_ref, mine_ref)

        return bad

    bad = jnp.sum(run(invert_fast))

    @pl.when(jnp.logical_not(bad < RESIDUE_LIMIT))
    def _():
        run(invert_safe)


def combine_kernel(weight_ref, offset_ref, mine_ref, partner_ref, third_a, third_b, pattern_ref, out_ref):
    _, core, _, _ = place()
    energy_count = lax.axis_size("energy")
    rank = lax.axis_index("energy")
    half = energy_count // 2
    near = rank + 1 - 2 * (rank % 2)
    away = 2 * rank - near
    far = (rank + half) % energy_count

    def weight_of(source):
        found = jnp.float32(0.0)
        for m in range(weight_ref.shape[0]):
            found = found + jnp.where(offset_ref[m] == rank - source, weight_ref[m], 0.0)
        return found

    near_weight = weight_of(near)
    far_weight = weight_of(far)
    away_weight = weight_of(away)
    mine_weight = jnp.where(core == 0, near_weight, far_weight)
    partner_weight = jnp.where(core == 0, far_weight, near_weight)
    keep = pattern_ref[...].astype(F32)
    for k in range(out_ref.shape[1]):
        for part in range(2):
            third = third_a[k, part] + third_b[k, part]
            value = mine_weight * mine_ref[k, part] + partner_weight * partner_ref[k, part] + away_weight * third
            out_ref[0, k, part] = value * keep


def kernel(body, shapes, smem=0, inputs=0):
    outs = [jax.ShapeDtypeStruct(s, F32) for s in shapes]
    specs = [pl.BlockSpec(memory_space=pltpu.SMEM)] * smem + [pl.BlockSpec(memory_space=pltpu.VMEM)] * inputs
    return pl.pallas_call(
        body,
        out_shape=outs if len(outs) > 1 else outs[0],
        in_specs=specs,
        out_specs=[pl.BlockSpec(memory_space=pltpu.VMEM)] * len(outs) if len(outs) > 1 else pl.BlockSpec(memory_space=pltpu.VMEM),
    )


def on_device(ham_diag, coupling, contact_left, mode_weight, mode_offset, pattern):
    n = ham_diag.shape[-1]
    assert ham_diag.shape[0] == 2
    space = lax.axis_size("space")
    energies = lax.axis_size("energy")
    chips = space // 2
    middle = chips // 2
    assert chips % 2 == 0 and space % 2 == 0 and energies % 4 == 0
    position = lax.axis_index("space")
    chip = position // 2
    depth = jnp.where(chip < middle, chip, chips - 1 - chip)
    swap = [(p, p ^ 1) for p in range(space)]

    ham_far = lax.ppermute(ham_diag, "space", swap)
    cpl_far = lax.ppermute(coupling, "space", swap)
    last = coupling[-1]
    before = [lax.ppermute(last, "space", [(2 * c + 1, 2 * c + 2 + k) for c in range(chips - 1)]) for k in range(2)]
    before = before[0] + before[1]

    blocks, links, ends, head = kernel(
        prepare_kernel, [(4, n, 2 * n), (6, n, 2 * n), (2, n, 2 * n), (n, 2 * n)], inputs=6
    )(
        ham_diag, ham_far, coupling, cpl_far, before, contact_left
    )
    state_shapes = [(RECORD, n, 2 * n), (n, 2 * n), (n, 2 * n)]
    forward = kernel(eliminate_kernel, state_shapes, inputs=3)
    state = forward(blocks, links, head)

    def chip_move(value, pairs):
        return lax.ppermute(value, "space", [(2 * a + k, 2 * b + k) for a, b in pairs for k in range(2)])

    head_of = kernel(head_kernel, [(n, 2 * n)], inputs=2)
    for d in range(1, middle):
        inward = [(c, c + 1) for c in range(middle - 1)] + [(c + 1, c) for c in range(middle, chips - 1)]
        fresh = forward(blocks, links, head_of(ends[0], chip_move(state[2], inward)))
        state = [jnp.where(depth >= d, a, b) for a, b in zip(fresh, state)]
    record, schur, corner = state

    message = chip_move(corner, [(middle - 1, middle), (middle, middle - 1)])
    spread = kernel(spread_kernel, [(9, n, 2 * n)], inputs=2)(links, record)
    for d in range(middle - 2, -1, -1):
        outward = [(c + 1, c) for c in range(middle - 1)] + [(c, c + 1) for c in range(middle, chips - 1)]
        back_links = jnp.concatenate([links[:2:-1], links[2::-1]], 0)
        fresh = forward(blocks[::-1], back_links, head_of(ends[1], message))
        message = jnp.where(depth == d, chip_move(fresh[2], outward), message)

    mine, theirs = kernel(finish_kernel, [(2, 2, n, n), (2, 2, n, n)], inputs=4)(schur, spread, ends, message)
    partner = lax.ppermute(theirs, "space", swap)

    def flat(p, e):
        return p * energies + e

    hops = [(e - 2, e) for e in range(2, energies, 2)] + [(e + 2, e) for e in range(1, energies - 2, 2)]
    third = [
        lax.ppermute(
            mine if k == 0 else theirs,
            ("space", "energy"),
            [(flat(2 * c, a), flat(2 * c + k, b)) for c in range(chips) for a, b in hops],
        )
        for k in range(2)
    ]
    return kernel(combine_kernel, [(1, 2, 2, n, n)], smem=2, inputs=5)(
        mode_weight, mode_offset, mine, partner, third[0], third[1], pattern
    )


def solution(mesh):
    placed = (P("space", None, None, None), P("space", None, None, None), P(), P(), P(), P())
    return jax.shard_map(
        on_device,
        mesh=mesh,
        in_specs=placed,
        out_specs=P("energy", "space", None, None, None),
        check_vma=False,
    )
```

```python
import functools
import math

import jax
import jax.numpy as jnp
from jax import lax
from jax.experimental import pallas as pl
from jax.experimental.pallas import tpu as pltpu
from jax.sharding import PartitionSpec as P

HIGHEST = lax.Precision.HIGHEST
BROADENING = 0.1
F32 = jnp.float32
BF16 = jnp.bfloat16


FULL_STEPS = 2
LOW_STEPS = 2
MOST_STEPS = 20
SETTLED = 0.999
RESIDUE_LIMIT = 4e-3
SAFE_STEPS = 64
KERNEL_VMEM = 24 << 20


def dot(a, b):
    return jnp.dot(a, b, preferred_element_type=F32)


def operand(b):
    n = b.shape[1] // 2
    return jnp.concatenate([b, jnp.concatenate([-b[:, n:], b[:, :n]], 1)], 0)


def halves(a):
    high = a.astype(BF16)
    return high, (a - high.astype(F32)).astype(BF16)


def mul_full(a, b):
    return jnp.dot(a, operand(b), precision=HIGHEST, preferred_element_type=F32)


def mul_split(a, b):
    a_high, a_low = halves(a)
    b_high, b_low = halves(b)
    b_high, b_low = operand(b_high), operand(b_low)
    return dot(a_high, b_high) + (dot(a_high, b_low) + dot(a_low, b_high))


def mul_low(a, b):
    return dot(a.astype(BF16), operand(b.astype(BF16)))


mul = mul_full


def adj(a):
    n = a.shape[1] // 2
    return jnp.concatenate([a[:, :n].T, -a[:, n:].T], 1)


def unit(n):
    row = lax.broadcasted_iota(jnp.int32, (n, 2 * n), 0)
    col = lax.broadcasted_iota(jnp.int32, (n, 2 * n), 1)
    return (row == col).astype(F32)


def times_half_imag(a):
    n = a.shape[1] // 2
    return jnp.concatenate([-0.5 * a[:, n:], 0.5 * a[:, :n]], 1)


def total(a):
    return jnp.sum(jnp.sum(a, axis=0, keepdims=True), axis=1, keepdims=True)


def start(a):
    back = adj(a)
    normal = mul_full(a, back)
    scale = 1.0 / jnp.sqrt(total(normal * normal))
    return back, normal, scale


def thresholds():
    value = SETTLED
    for _ in range(MOST_STEPS):
        yield value
        value = value / (2.0 - value + 2.0 * math.sqrt(1.0 - value))


def invert_fast(mats):
    n = mats[0].shape[0]
    one = unit(n)
    state = []
    lowest = None
    for a in mats:
        back, normal, scale = start(a)
        least = (0.99 * BROADENING**2) * scale
        lowest = least if lowest is None else jnp.minimum(lowest, least)
        state.append((back, one - normal * scale, least, scale))
    lowest = lowest[0, 0]
    count = jnp.int32(0)
    for value in thresholds():
        count = count + (lowest < value).astype(jnp.int32)

    def step(multiply, _, state):
        fresh = []
        for x, rest, least, gain in state:
            c = 2.0 / (1.0 + least)
            centred = (1.0 - c) * one + c * rest
            both = multiply(jnp.concatenate([x, centred], 0), centred)
            fresh.append((x + both[:n], both[n:], jnp.minimum(c * c * least, 1.0), c * gain))
        return tuple(fresh)

    state = tuple(state)
    for k in range(FULL_STEPS):
        state = step(mul_full, k, state)
    middle = jnp.maximum(count - (FULL_STEPS + LOW_STEPS), 0)
    state = lax.fori_loop(0, middle, functools.partial(step, mul_split), state)
    state = lax.fori_loop(0, LOW_STEPS, functools.partial(step, mul_low), state)
    found, worst = [], jnp.zeros((1, 1), F32)
    for a, (x, _, _, gain) in zip(mats, state):
        x = x * gain
        residue = one - mul_full(a, x)
        worst = jnp.maximum(worst, total(residue * residue))
        found.append(x + mul_split(x, residue))
    return found, worst


def invert_safe(mats):
    n = mats[0].shape[0]
    one = unit(n)
    found = []
    for a in mats:
        back, _, scale = start(a)

        def step(_, x):
            return x + mul_full(x, one - mul_full(a, x))

        x = lax.fori_loop(0, SAFE_STEPS, step, back * scale)
        found.append(x)
    return found, jnp.zeros((1, 1), F32)


def row_form(ref, index=None):
    if index is None:
        return jnp.concatenate([ref[0], ref[1]], 1)
    return jnp.concatenate([ref[index, 0], ref[index, 1]], 1)


def place():
    position = lax.axis_index("space")
    chip = position // 2
    core = position % 2
    right = (chip >= lax.axis_size("space") // 4).astype(jnp.int32)
    outer = (core == right).astype(jnp.int32)
    return position, core, right, outer


def load(pairs, sems):
    copies = [pltpu.make_async_copy(src, dst, sems.at[k]) for k, (src, dst) in enumerate(pairs)]
    for copy in copies:
        copy.start()
    return copies


def prepared(ham, cpl):
    n = ham.shape[-1]
    _, core, _, _ = place()
    energy_count = lax.axis_size("energy")
    rank = lax.axis_index("energy")
    near = rank + 1 - 2 * (rank % 2)
    solved = jnp.where(core == 0, near, (rank + energy_count // 2) % energy_count)
    energy = -2.0 + (solved.astype(F32) + 0.5) * (4.0 / energy_count)
    one = unit(n)
    shift = energy * one + BROADENING * jnp.concatenate([one[:, n:], one[:, :n]], 1)
    hams = [row_form(ham, k) for k in range(2)]
    links = [row_form(cpl, k) for k in range(2)]
    return [shift - 0.5 * (m + adj(m)) for m in hams], links, [adj(m) for m in links]


BACK, CONTACT, LINKS = 4, 8, 10


def block_index(k):
    _, _, right, outer = place()
    return (2 * (1 - outer) if k < 2 else 2 * outer) + (k % 2 + right * (1 - 2 * (k % 2)))


def chip_index(j, core):
    return (2 * core if j < 2 else 2 * (1 - core)) + j % 2


def link_index(k):
    _, core, right, _ = place()
    at = jnp.where(right == 1, chip_index(2 - k, core), chip_index(k, core))
    return at + BACK * right, at + BACK * (1 - right)


def fill(ham, cpl, base, blocks_ref, links_ref):
    blocks, links, backs = prepared(ham, cpl)
    for k in range(2):
        blocks_ref[base + k] = blocks[k]
        links_ref[base + k] = links[k]
        links_ref[BACK + base + k] = backs[k]


def own_kernel(ham_hbm, cpl_hbm, contact_hbm, blocks_ref, links_ref, ham, cpl, contact, sems):
    for copy in load([(ham_hbm, ham), (cpl_hbm, cpl), (contact_hbm, contact)], sems):
        copy.wait()
    fill(ham, cpl, 0, blocks_ref, links_ref)
    lead = row_form(contact)
    links_ref[CONTACT] = lead
    links_ref[CONTACT + 1] = adj(lead)


def join_kernel(own_blocks, own_links, ham, cpl, blocks_ref, links_ref, head_ref, last_ref):
    _, core, right, _ = place()
    fill(ham, cpl, 2, blocks_ref, links_ref)
    end = chip_index(3, core)
    lead = links_ref[jnp.where(right == 1, BACK + end, CONTACT)]
    lead_back = links_ref[jnp.where(right == 1, end, CONTACT + 1)]
    last_ref[...] = links_ref[end]
    head_ref[...] = times_half_imag(mul(lead, lead_back))


B0, B1, B2, T0, P1, P2, Q, R, RECORD = range(9)


def chain_links(turned):
    found = [link_index(k) for k in range(3)]
    if turned:
        found = [(b, a) for a, b in found[::-1]]
    return [a for a, _ in found] + [b for _, b in found]


def eliminate(blocks, links, head, record, schur_ref, corner_ref, invert):
    c0, c1, c2, c0h, c1h, c2h = links
    (b0, b2), bad = invert([blocks[0] + head, blocks[2]])
    t0 = mul(b0, c0)
    p1 = mul(b2, c1h)
    p2 = mul(b2, c2)
    record[B0], record[B2], record[T0], record[P1], record[P2] = b0, b2, t0, p1, p2
    middle = blocks[1] - mul(c0h, t0) - mul(c1, p1)
    upper = mul(c1, p2)
    lower = mul(c2h, p1)
    tail = blocks[3] - mul(c2h, p2)
    (b1,), more = invert([middle])
    bad = jnp.maximum(bad, more)
    q = mul(b1, upper)
    r = mul(lower, b1)
    schur = tail - mul(lower, q)
    record[B1], record[Q], record[R] = b1, q, r
    schur_ref[...] = schur
    (corner,), more = invert([schur])
    corner_ref[...] = corner
    return jnp.maximum(bad, more)


def chip_ends(links_ref, before_ref):
    _, core, right, _ = place()
    ahead = before_ref[...]
    back = adj(ahead)
    end = chip_index(3, core)
    last, last_back = links_ref[end], links_ref[BACK + end]
    mirrored = right == 1
    pick = lambda a, b: jnp.where(mirrored, a, b)
    return [pick(last, back), pick(last_back, ahead), pick(back, last), pick(ahead, last_back)]


def ends_kernel(links_ref, before_ref, out_ref):
    for k, value in enumerate(chip_ends(links_ref, before_ref)):
        out_ref[k] = value


def head_kernel(link_ref, back_ref, message_ref, out_ref):
    out_ref[...] = -mul(mul(link_ref[...], message_ref[...]), back_ref[...])


def eliminate_kernel(turned, blocks_ref, links_ref, head_ref, record_ref, schur_ref, corner_ref):
    def run(invert):
        return eliminate(
            [blocks_ref[block_index(3 - k if turned else k)] for k in range(4)],
            [links_ref[at] for at in chain_links(turned)],
            head_ref[...],
            record_ref,
            schur_ref,
            corner_ref,
            invert,
        )

    bad = jnp.sum(run(invert_fast))

    @pl.when(jnp.logical_not(bad < RESIDUE_LIMIT))
    def _():
        run(invert_safe)


def spread_kernel(links_ref, record_ref, before_ref, out_ref):
    c0, c1, _, c0h, _, c2h = (links_ref[at] for at in chain_links(False))
    b0, b1, b2, t0, p1, p2, q, r = (record_ref[k] for k in range(RECORD))
    w0 = mul(c0h, b0)
    m1 = mul(c1, b2)
    m2 = mul(c2h, b2)
    out_ref[0] = b0 + mul(mul(t0, b1), w0)
    out_ref[1] = b1
    out_ref[2] = b2 + mul(mul(p1, b1), m1)
    out_ref[3] = mul(t0, q)
    out_ref[4] = q
    out_ref[5] = mul(p1, q) + p2
    out_ref[6] = mul(r, w0)
    out_ref[7] = r
    out_ref[8] = mul(r, m1) + m2
    _, _, out_ref[9], out_ref[10] = chip_ends(links_ref, before_ref)


def finish_kernel(schur_ref, spread_ref, message_ref, mine_ref, theirs_ref):
    _, core, right, outer = place()
    n = schur_ref.shape[0]

    def run(invert):
        closed = schur_ref[...] - mul(mul(spread_ref[9], message_ref[...]), spread_ref[10])
        (full,), bad = invert([closed])
        reach = mul(jnp.concatenate([spread_ref[3 + j] for j in range(3)], 0), full)
        green = [spread_ref[j] + mul(reach[j * n : (j + 1) * n], spread_ref[6 + j]) for j in range(3)] + [full]

        def store(outer_ref, inner_ref):
            for k in range(4):
                ref = outer_ref if k < 2 else inner_ref
                index = jnp.where(right == 1, 1 - k % 2, k % 2)
                ref[index, 0] = green[k][:, :n]
                ref[index, 1] = green[k][:, n:]

        @pl.when(outer == 1)
        def _():
            store(mine_ref, theirs_ref)

        @pl.when(outer == 0)
        def _():
            store(theirs_ref, mine_ref)

        return bad

    bad = jnp.sum(run(invert_fast))

    @pl.when(jnp.logical_not(bad < RESIDUE_LIMIT))
    def _():
        run(invert_safe)


def combine_kernel(
    weight_ref, offset_ref, mine_ref, partner_ref, third_a, third_b, pattern_hbm, out_ref, pattern_ref, sem
):
    _, core, _, _ = place()
    pltpu.sync_copy(pattern_hbm, pattern_ref)
    energy_count = lax.axis_size("energy")
    rank = lax.axis_index("energy")
    half = energy_count // 2
    near = rank + 1 - 2 * (rank % 2)
    away = 2 * rank - near
    far = (rank + half) % energy_count

    def weight_of(source):
        found = jnp.float32(0.0)
        for m in range(weight_ref.shape[0]):
            found = found + jnp.where(offset_ref[m] == rank - source, weight_ref[m], 0.0)
        return found

    near_weight = weight_of(near)
    far_weight = weight_of(far)
    away_weight = weight_of(away)
    mine_weight = jnp.where(core == 0, near_weight, far_weight)
    partner_weight = jnp.where(core == 0, far_weight, near_weight)
    keep = pattern_ref[...].astype(F32)
    for k in range(out_ref.shape[1]):
        for part in range(2):
            value = mine_weight * mine_ref[k, part] + partner_weight * partner_ref[k, part]
            value = value + away_weight * jnp.where(core == 0, third_a[k, part], third_b[k, part])
            out_ref[0, k, part] = value * keep


def kernel(body, shapes, where, scratch=(), aliases=None, result="v"):
    spaces = {"s": pltpu.SMEM, "v": pltpu.VMEM, "a": pl.ANY}
    many = len(shapes) > 1
    if result == "v":
        outs = [pltpu.VMEM(shape, F32) for shape in shapes]
    else:
        outs = [jax.ShapeDtypeStruct(shape, F32) for shape in shapes]
    out_specs = [pl.BlockSpec(memory_space=pltpu.VMEM) for _ in shapes]
    call = pl.pallas_call(
        body,
        out_shape=outs if many else outs[0],
        in_specs=[pl.BlockSpec(memory_space=spaces[w]) for w in where],
        out_specs=out_specs if many else out_specs[0],
        scratch_shapes=list(scratch),
        input_output_aliases=aliases or {},
        compiler_params=pltpu.CompilerParams(vmem_limit_bytes=KERNEL_VMEM),
    )

    def placed(*operands):
        return call(*(
            pltpu.with_memory_space_constraint(x, pltpu.VMEM) if w == "v" else x for x, w in zip(operands, where)
        ))

    return placed


def on_device(ham_diag, coupling, contact_left, mode_weight, mode_offset, pattern):
    n = ham_diag.shape[-1]
    assert ham_diag.shape[0] == 2
    space = lax.axis_size("space")
    energies = lax.axis_size("energy")
    chips = space // 2
    middle = chips // 2
    assert chips % 2 == 0 and space % 2 == 0 and energies % 4 == 0
    position = lax.axis_index("space")
    chip = position // 2
    depth = jnp.where(chip < middle, chip, chips - 1 - chip)
    swap = [(p, p ^ 1) for p in range(space)]

    row = (n, 2 * n)
    pair = (2, 2, n, n)
    vmem = lambda *shape: pltpu.VMEM(shape, F32)
    sems = lambda count: pltpu.SemaphoreType.DMA((count,))

    ham_far = lax.ppermute(ham_diag, "space", swap)
    cpl_far = lax.ppermute(coupling, "space", swap)

    own = kernel(
        own_kernel, [(4,) + row, (LINKS,) + row], "aaa", [vmem(*pair), vmem(*pair), vmem(2, n, n), sems(3)]
    )(ham_diag, coupling, contact_left)
    blocks, links, head, last = kernel(
        join_kernel, [(4,) + row, (LINKS,) + row, row, row], "vvvv", aliases={0: 0, 1: 1}
    )(*own, ham_far, cpl_far)
    forward, backward = (
        kernel(functools.partial(eliminate_kernel, turned), [(RECORD,) + row, row, row], "vvv")
        for turned in (False, True)
    )
    def chip_move(value, pairs):
        return lax.ppermute(value, "space", [(2 * a + k, 2 * b + k) for a, b in pairs for k in range(2)])

    before = chip_move(last, [(c, c + 1) for c in range(chips - 1)])
    state = forward(blocks, links, head)

    if middle > 1:
        ends = kernel(ends_kernel, [(4,) + row], "vv")(links, before)
        head_of = kernel(head_kernel, [row], "vvv")
    for d in range(1, middle):
        inward = [(c, c + 1) for c in range(middle - 1)] + [(c + 1, c) for c in range(middle, chips - 1)]
        fresh = forward(blocks, links, head_of(ends[0], ends[1], chip_move(state[2], inward)))
        state = [jnp.where(depth >= d, a, b) for a, b in zip(fresh, state)]
    record, schur, corner = state

    message = chip_move(corner, [(middle - 1, middle), (middle, middle - 1)])
    spread = kernel(spread_kernel, [(11,) + row], "vvv")(links, record, before)
    for d in range(middle - 2, -1, -1):
        outward = [(c + 1, c) for c in range(middle - 1)] + [(c, c + 1) for c in range(middle, chips - 1)]
        fresh = backward(blocks, links, head_of(ends[2], ends[3], message))
        message = jnp.where(depth == d, chip_move(fresh[2], outward), message)

    mine, theirs = kernel(finish_kernel, [pair, pair], "vvv")(schur, spread, message)
    partner = lax.ppermute(theirs, "space", swap)

    def flat(p, e):
        return p * energies + e

    hops = [(e - 2, e) for e in range(2, energies, 2)] + [(e + 2, e) for e in range(1, energies - 2, 2)]
    third = [
        lax.ppermute(
            mine if k == 0 else theirs,
            ("space", "energy"),
            [(flat(2 * c, a), flat(2 * c + k, b)) for c in range(chips) for a, b in hops],
        )
        for k in range(2)
    ]
    return kernel(
        combine_kernel, [(1,) + pair], "ssvvvva", [pltpu.VMEM(pattern.shape, jnp.int32), sems(1)], result="a"
    )(mode_weight, mode_offset, mine, partner, third[0], third[1], pattern)


def solution(mesh):
    placed = (P("space", None, None, None), P("space", None, None, None), P(), P(), P(), P())
    return jax.shard_map(
        on_device,
        mesh=mesh,
        in_specs=placed,
        out_specs=P("energy", "space", None, None, None),
        check_vma=False,
    )
```

```python
import functools
import math

import jax
import jax.numpy as jnp
from jax import lax
from jax.experimental import pallas as pl
from jax.experimental.pallas import tpu as pltpu
from jax.sharding import PartitionSpec as P


HIGHEST = lax.Precision.HIGHEST
BROADENING = 0.1
F32 = jnp.float32
BF16 = jnp.bfloat16


LATE_STEPS = 2
MOST_STEPS = 20
SETTLED = 0.999
RESIDUE_LIMIT = 4e-3
SAFE_STEPS = 64
KERNEL_VMEM = 24 << 20


def dot(a, b):
    return jnp.dot(a, b, preferred_element_type=F32)


def operand(b):
    n = b.shape[1] // 2
    return jnp.concatenate([b, jnp.concatenate([-b[:, n:], b[:, :n]], 1)], 0)


def halves(a):
    high = a.astype(BF16)
    return high, (a - high.astype(F32)).astype(BF16)


def mul_full(a, b):
    return jnp.dot(a, operand(b), precision=HIGHEST, preferred_element_type=F32)


def mul_split(a, b):
    a_high, a_low = halves(a)
    b_high, b_low = halves(b)
    b_high, b_low = operand(b_high), operand(b_low)
    return dot(a_high, b_high) + (dot(a_high, b_low) + dot(a_low, b_high))


def mul_low(a, b):
    return dot(a.astype(BF16), operand(b.astype(BF16)))


mul = mul_full


def adj(a):
    n = a.shape[1] // 2
    return jnp.concatenate([a[:, :n].T, -a[:, n:].T], 1)


def unit(n):
    row = lax.broadcasted_iota(jnp.int32, (n, 2 * n), 0)
    col = lax.broadcasted_iota(jnp.int32, (n, 2 * n), 1)
    return (row == col).astype(F32)


def times_half_imag(a):
    n = a.shape[1] // 2
    return jnp.concatenate([-0.5 * a[:, n:], 0.5 * a[:, :n]], 1)


def total(a):
    return jnp.sum(jnp.sum(a, axis=0, keepdims=True), axis=1, keepdims=True)


def start(a):
    back = adj(a)
    normal = mul_full(a, back)
    scale = 1.0 / jnp.sqrt(total(normal * normal))
    return back, normal, scale


def thresholds():
    value = SETTLED
    for _ in range(MOST_STEPS):
        yield value
        value = value / (2.0 - value + 2.0 * math.sqrt(1.0 - value))


def early_step(_, state):
    fresh = []
    for x, d, least, gain in state:
        n = d.shape[0]
        c = 2.0 / (1.0 + least)
        both = mul_split(jnp.concatenate([d, x], 0), d)
        fresh.append((2.0 * x - c * both[n:], c * (2.0 * d - c * both[:n]), jnp.minimum(c * c * least, 1.0), c * gain))
    return tuple(fresh)


def late_step(state):
    fresh = []
    for x, rest, least, gain in state:
        n = rest.shape[0]
        c = 2.0 / (1.0 + least)
        centred = (1.0 - c) * unit(n) + c * rest
        both = mul_low(jnp.concatenate([centred, x], 0), centred)
        fresh.append((x + both[n:], both[:n], jnp.minimum(c * c * least, 1.0), c * gain))
    return tuple(fresh)


def invert_fast(mats):
    state = []
    lowest = None
    for a in mats:
        back, normal, scale = start(a)
        least = (0.99 * BROADENING**2) * scale
        lowest = least if lowest is None else jnp.minimum(lowest, least)
        state.append((back, normal * scale, least, scale))
    lowest = lowest[0, 0]
    count = jnp.int32(0)
    for value in thresholds():
        count = count + (lowest < value).astype(jnp.int32)
    state = lax.fori_loop(0, jnp.maximum(count - LATE_STEPS, 0), early_step, tuple(state))
    one = unit(mats[0].shape[0])
    state = tuple((x, one - d, least, gain) for x, d, least, gain in state)
    for _ in range(LATE_STEPS):
        state = late_step(state)
    found, worst = [], jnp.zeros((1, 1), F32)
    for a, (x, _, _, gain) in zip(mats, state):
        x = x * gain
        residue = one - mul_full(a, x)
        worst = jnp.maximum(worst, total(residue * residue))
        found.append(x + mul_split(x, residue))
    return found, worst


def invert_safe(mats):
    n = mats[0].shape[0]
    one = unit(n)
    found = []
    for a in mats:
        back, _, scale = start(a)

        def step(_, x):
            return x + mul_full(x, one - mul_full(a, x))

        x = lax.fori_loop(0, SAFE_STEPS, step, back * scale)
        found.append(x)
    return found, jnp.zeros((1, 1), F32)


def row_form(ref, index=None):
    if index is None:
        return jnp.concatenate([ref[0], ref[1]], 1)
    return jnp.concatenate([ref[index, 0], ref[index, 1]], 1)


def place():
    position = lax.axis_index("space")
    chip = position // 2
    core = position % 2
    right = (chip >= lax.axis_size("space") // 4).astype(jnp.int32)
    outer = (core == right).astype(jnp.int32)
    return position, core, right, outer


def load(pairs, sems):
    copies = [pltpu.make_async_copy(src, dst, sems.at[k]) for k, (src, dst) in enumerate(pairs)]
    for copy in copies:
        copy.start()
    return copies


def prepared(ham, cpl):
    n = ham.shape[-1]
    _, core, _, _ = place()
    energy_count = lax.axis_size("energy")
    rank = lax.axis_index("energy")
    near = rank + 1 - 2 * (rank % 2)
    solved = jnp.where(core == 0, near, (rank + energy_count // 2) % energy_count)
    energy = -2.0 + (solved.astype(F32) + 0.5) * (4.0 / energy_count)
    one = unit(n)
    shift = energy * one + BROADENING * jnp.concatenate([one[:, n:], one[:, :n]], 1)
    hams = [row_form(ham, k) for k in range(2)]
    links = [row_form(cpl, k) for k in range(2)]
    return [shift - 0.5 * (m + adj(m)) for m in hams], links, [adj(m) for m in links]


BACK, CONTACT, LINKS = 4, 8, 10


def block_index(k):
    _, _, right, outer = place()
    return (2 * (1 - outer) if k < 2 else 2 * outer) + (k % 2 + right * (1 - 2 * (k % 2)))


def chip_index(j, core):
    return (2 * core if j < 2 else 2 * (1 - core)) + j % 2


def link_index(k):
    _, core, right, _ = place()
    at = jnp.where(right == 1, chip_index(2 - k, core), chip_index(k, core))
    return at + BACK * right, at + BACK * (1 - right)


def fill(ham, cpl, base, blocks_ref, links_ref):
    blocks, links, backs = prepared(ham, cpl)
    for k in range(2):
        blocks_ref[base + k] = blocks[k]
        links_ref[base + k] = links[k]
        links_ref[BACK + base + k] = backs[k]


def own_kernel(ham_hbm, cpl_hbm, contact_hbm, blocks_ref, links_ref, ham, cpl, contact, sems):
    for copy in load([(ham_hbm, ham), (cpl_hbm, cpl), (contact_hbm, contact)], sems):
        copy.wait()
    fill(ham, cpl, 0, blocks_ref, links_ref)
    lead = row_form(contact)
    links_ref[CONTACT] = lead
    links_ref[CONTACT + 1] = adj(lead)


def join_kernel(own_blocks, own_links, ham, cpl, blocks_ref, links_ref, head_ref, last_ref):
    _, core, right, _ = place()
    fill(ham, cpl, 2, blocks_ref, links_ref)
    end = chip_index(3, core)
    lead = links_ref[jnp.where(right == 1, BACK + end, CONTACT)]
    lead_back = links_ref[jnp.where(right == 1, end, CONTACT + 1)]
    last_ref[...] = links_ref[end]
    head_ref[...] = times_half_imag(mul(lead, lead_back))


B0, B1, B2, T0, P1, P2, Q, R, RECORD = range(9)


def chain_links(turned):
    found = [link_index(k) for k in range(3)]
    if turned:
        found = [(b, a) for a, b in found[::-1]]
    return [a for a, _ in found] + [b for _, b in found]


def eliminate(blocks, links, head, record, schur_ref, corner_ref, invert):
    c0, c1, c2, c0h, c1h, c2h = links
    (b0, b2), bad = invert([blocks[0] + head, blocks[2]])
    t0 = mul(b0, c0)
    p1 = mul(b2, c1h)
    p2 = mul(b2, c2)
    record[B0], record[B2], record[T0], record[P1], record[P2] = b0, b2, t0, p1, p2
    middle = blocks[1] - mul(c0h, t0) - mul(c1, p1)
    upper = mul(c1, p2)
    lower = mul(c2h, p1)
    tail = blocks[3] - mul(c2h, p2)
    (b1,), more = invert([middle])
    bad = jnp.maximum(bad, more)
    q = mul(b1, upper)
    r = mul(lower, b1)
    schur = tail - mul(lower, q)
    record[B1], record[Q], record[R] = b1, q, r
    schur_ref[...] = schur
    (corner,), more = invert([schur])
    corner_ref[...] = corner
    return jnp.maximum(bad, more)


def chip_ends(links_ref, before_ref):
    _, core, right, _ = place()
    ahead = before_ref[...]
    back = adj(ahead)
    end = chip_index(3, core)
    last, last_back = links_ref[end], links_ref[BACK + end]
    mirrored = right == 1
    pick = lambda a, b: jnp.where(mirrored, a, b)
    return [pick(last, back), pick(last_back, ahead), pick(back, last), pick(ahead, last_back)]


def ends_kernel(links_ref, before_ref, out_ref):
    for k, value in enumerate(chip_ends(links_ref, before_ref)):
        out_ref[k] = value


def head_kernel(link_ref, back_ref, message_ref, out_ref):
    out_ref[...] = -mul(mul(link_ref[...], message_ref[...]), back_ref[...])


def eliminate_kernel(turned, blocks_ref, links_ref, head_ref, record_ref, schur_ref, corner_ref):
    def run(invert):
        return eliminate(
            [blocks_ref[block_index(3 - k if turned else k)] for k in range(4)],
            [links_ref[at] for at in chain_links(turned)],
            head_ref[...],
            record_ref,
            schur_ref,
            corner_ref,
            invert,
        )

    bad = jnp.sum(run(invert_fast))

    @pl.when(jnp.logical_not(bad < RESIDUE_LIMIT))
    def _():
        run(invert_safe)


def spread_kernel(links_ref, record_ref, before_ref, out_ref):
    _, c1, _, c0h, _, c2h = (links_ref[at] for at in chain_links(False))
    b0, b1, b2, t0, p1, p2, q, r = (record_ref[k] for k in range(RECORD))
    w0 = mul(c0h, b0)
    m1 = mul(c1, b2)
    m2 = mul(c2h, b2)
    out_ref[0] = b0 + mul(mul(t0, b1), w0)
    out_ref[1] = b1
    out_ref[2] = b2 + mul(mul(p1, b1), m1)
    out_ref[3] = mul(t0, q)
    out_ref[4] = q
    out_ref[5] = mul(p1, q) + p2
    out_ref[6] = mul(r, w0)
    out_ref[7] = r
    out_ref[8] = mul(r, m1) + m2
    _, _, out_ref[9], out_ref[10] = chip_ends(links_ref, before_ref)


def finish_kernel(schur_ref, spread_ref, message_ref, mine_ref, theirs_ref):
    _, _, right, outer = place()
    n = schur_ref.shape[0]

    def run(invert):
        closed = schur_ref[...] - mul(mul(spread_ref[9], message_ref[...]), spread_ref[10])
        (full,), bad = invert([closed])
        reach = mul_split(jnp.concatenate([spread_ref[3 + j] for j in range(3)], 0), full)
        green = [spread_ref[j] + mul_split(reach[j * n : (j + 1) * n], spread_ref[6 + j]) for j in range(3)] + [full]

        def store(outer_ref, inner_ref):
            for k in range(4):
                ref = outer_ref if k < 2 else inner_ref
                index = jnp.where(right == 1, 1 - k % 2, k % 2)
                ref[index, 0] = green[k][:, :n]
                ref[index, 1] = green[k][:, n:]

        @pl.when(outer == 1)
        def _():
            store(mine_ref, theirs_ref)

        @pl.when(outer == 0)
        def _():
            store(theirs_ref, mine_ref)

        return bad

    bad = jnp.sum(run(invert_fast))

    @pl.when(jnp.logical_not(bad < RESIDUE_LIMIT))
    def _():
        run(invert_safe)


def combine_kernel(
    weight_ref, offset_ref, mine_ref, partner_ref, third_ref, pattern_hbm, out_ref, pattern_ref, sem
):
    _, core, _, _ = place()
    pltpu.sync_copy(pattern_hbm, pattern_ref)
    energy_count = lax.axis_size("energy")
    rank = lax.axis_index("energy")
    half = energy_count // 2
    near = rank + 1 - 2 * (rank % 2)
    away = 2 * rank - near
    far = (rank + half) % energy_count

    def weight_of(source):
        found = jnp.float32(0.0)
        for m in range(weight_ref.shape[0]):
            found = found + jnp.where(offset_ref[m] == rank - source, weight_ref[m], 0.0)
        return found

    near_weight = weight_of(near)
    far_weight = weight_of(far)
    away_weight = weight_of(away)
    mine_weight = jnp.where(core == 0, near_weight, far_weight)
    partner_weight = jnp.where(core == 0, far_weight, near_weight)
    keep = pattern_ref[...].astype(F32)
    for k in range(out_ref.shape[1]):
        for part in range(2):
            value = mine_weight * mine_ref[k, part] + partner_weight * partner_ref[k, part]
            value = value + away_weight * third_ref[k, part]
            out_ref[0, k, part] = value * keep


def kernel(body, shapes, where, scratch=(), aliases=None, result="v"):
    spaces = {"s": pltpu.SMEM, "v": pltpu.VMEM, "a": pl.ANY, "h": pltpu.HBM}
    many = len(shapes) > 1
    if result == "v":
        outs = [pltpu.VMEM(shape, F32) for shape in shapes]
    else:
        outs = [jax.ShapeDtypeStruct(shape, F32) for shape in shapes]
    out_specs = [pl.BlockSpec(memory_space=pltpu.VMEM) for _ in shapes]
    call = pl.pallas_call(
        body,
        out_shape=outs if many else outs[0],
        in_specs=[pl.BlockSpec(memory_space=spaces[w]) for w in where],
        out_specs=out_specs if many else out_specs[0],
        scratch_shapes=list(scratch),
        input_output_aliases=aliases or {},
        compiler_params=pltpu.CompilerParams(vmem_limit_bytes=KERNEL_VMEM),
    )

    def placed(*operands):
        return call(*(
            pltpu.with_memory_space_constraint(x, spaces[w]) if w in "vh" else x for x, w in zip(operands, where)
        ))

    return placed


def on_device(ham_diag, coupling, contact_left, mode_weight, mode_offset, pattern):
    n = ham_diag.shape[-1]
    assert ham_diag.shape[0] == 2
    space = lax.axis_size("space")
    energies = lax.axis_size("energy")
    chips = space // 2
    middle = chips // 2
    assert chips % 2 == 0 and space % 2 == 0 and energies % 4 == 0
    position = lax.axis_index("space")
    chip = position // 2
    depth = jnp.where(chip < middle, chip, chips - 1 - chip)
    swap = [(p, p ^ 1) for p in range(space)]

    row = (n, 2 * n)
    pair = (2, 2, n, n)
    vmem = lambda *shape: pltpu.VMEM(shape, F32)
    sems = lambda count: pltpu.SemaphoreType.DMA((count,))

    ham_far = lax.ppermute(ham_diag, "space", swap)
    cpl_far = lax.ppermute(coupling, "space", swap)

    own = kernel(
        own_kernel, [(4,) + row, (LINKS,) + row], "hhh", [vmem(*pair), vmem(*pair), vmem(2, n, n), sems(3)]
    )(ham_diag, coupling, contact_left)
    blocks, links, head, last = kernel(
        join_kernel, [(4,) + row, (LINKS,) + row, row, row], "vvvv", aliases={0: 0, 1: 1}
    )(*own, ham_far, cpl_far)
    forward, backward = (
        kernel(functools.partial(eliminate_kernel, turned), [(RECORD,) + row, row, row], "vvv")
        for turned in (False, True)
    )

    def chip_move(value, pairs):
        return lax.ppermute(value, "space", [(2 * a + k, 2 * b + k) for a, b in pairs for k in range(2)])

    before = chip_move(last, [(c, c + 1) for c in range(chips - 1)])
    state = forward(blocks, links, head)

    if middle > 1:
        ends = kernel(ends_kernel, [(4,) + row], "vv")(links, before)
        head_of = kernel(head_kernel, [row], "vvv")
    for d in range(1, middle):
        inward = [(c, c + 1) for c in range(middle - 1)] + [(c + 1, c) for c in range(middle, chips - 1)]
        fresh = forward(blocks, links, head_of(ends[0], ends[1], chip_move(state[2], inward)))
        state = [jnp.where(depth >= d, a, b) for a, b in zip(fresh, state)]
    record, schur, corner = state

    message = chip_move(corner, [(middle - 1, middle), (middle, middle - 1)])
    spread = kernel(spread_kernel, [(11,) + row], "vvv")(links, record, before)
    for d in range(middle - 2, -1, -1):
        outward = [(c + 1, c) for c in range(middle - 1)] + [(c, c + 1) for c in range(middle, chips - 1)]
        fresh = backward(blocks, links, head_of(ends[2], ends[3], message))
        message = jnp.where(depth == d, chip_move(fresh[2], outward), message)

    mine, theirs = kernel(finish_kernel, [pair, pair], "vvv")(schur, spread, message)
    ends_from = [(e + 1 - 2 * (1 - e % 2), e) for e in range(energies)]
    wanted = [(source, e) for source, e in ends_from if 0 <= source < energies]
    pairs = []
    for c in range(chips):
        for source, e in wanted:
            for k, site in enumerate((source + 1 - 2 * (source % 2), (source + energies // 2) % energies)):
                pairs.append(((2 * c + k) * energies + site, (2 * c + k) * energies + e))
    third = lax.ppermute(mine, ("space", "energy"), pairs)
    partner = lax.ppermute(theirs, "space", swap)
    return kernel(
        combine_kernel, [(1,) + pair], "ssvvva", [pltpu.VMEM(pattern.shape, jnp.int32), sems(1)], result="a"
    )(mode_weight, mode_offset, mine, partner, third, pattern)


def solution(mesh):
    placed = (P("space", None, None, None), P("space", None, None, None), P(), P(), P(), P())
    return jax.shard_map(
        on_device,
        mesh=mesh,
        in_specs=placed,
        out_specs=P("energy", "space", None, None, None),
        check_vma=False,
    )
```

```python
import functools
import math

import jax
import jax.numpy as jnp
from jax import lax
from jax.experimental import pallas as pl
from jax.experimental.pallas import tpu as pltpu
from jax.sharding import PartitionSpec as P


HIGHEST = lax.Precision.HIGHEST
BROADENING = 0.1
F32 = jnp.float32
BF16 = jnp.bfloat16


FIXED_STEPS = (8, 7)
LATE_STEPS = 2
MOST_STEPS = 20
SETTLED = 0.999
RESIDUE_LIMIT = 4e-3
SAFE_STEPS = 64
KERNEL_VMEM = 24 << 20


def dot(a, b):
    return jnp.dot(a, b, preferred_element_type=F32)


def operand(b):
    n = b.shape[1] // 2
    return jnp.concatenate([b, jnp.concatenate([-b[:, n:], b[:, :n]], 1)], 0)


def halves(a):
    high = a.astype(BF16)
    return high, (a - high.astype(F32)).astype(BF16)


def mul_full(a, b):
    return jnp.dot(a, operand(b), precision=HIGHEST, preferred_element_type=F32)


def mul_split(a, b):
    m = a.shape[0]
    a_high, a_low = halves(a)
    b_high, b_low = halves(b)
    b_high, b_low = operand(b_high), operand(b_low)
    both = dot(jnp.concatenate([a_high, a_low], 0), b_high)
    return both[:m] + (both[m:] + dot(a_high, b_low))


def mul_low(a, b):
    return dot(a.astype(BF16), operand(b.astype(BF16)))


mul = mul_full


def adj(a):
    n = a.shape[1] // 2
    return jnp.concatenate([a[:, :n].T, -a[:, n:].T], 1)


def unit(n):
    row = lax.broadcasted_iota(jnp.int32, (n, 2 * n), 0)
    col = lax.broadcasted_iota(jnp.int32, (n, 2 * n), 1)
    return (row == col).astype(F32)


def times_half_imag(a):
    n = a.shape[1] // 2
    return jnp.concatenate([-0.5 * a[:, n:], 0.5 * a[:, :n]], 1)


def total(a):
    return jnp.sum(jnp.sum(a, axis=0, keepdims=True), axis=1, keepdims=True)


def start(a):
    n = a.shape[0]
    back = adj(a)
    normal = mul_split(a, back)
    size = jnp.sqrt(a[:, :n] * a[:, :n] + a[:, n:] * a[:, n:])
    across = jnp.max(jnp.sum(size, axis=1, keepdims=True), axis=0, keepdims=True)
    down = jnp.max(jnp.sum(size, axis=0, keepdims=True), axis=1, keepdims=True)
    return back, normal, 1.0 / (across * down)


def thresholds():
    value = SETTLED
    for _ in range(MOST_STEPS):
        yield value
        value = value / (2.0 - value + 2.0 * math.sqrt(1.0 - value))


def early_step(_, state):
    fresh = []
    for x, d, least, gain in state:
        c = 2.0 / (1.0 + least)
        square = mul_split(d, d)
        x = 2.0 * x - c * mul_split(x, d)
        fresh.append((x, c * (2.0 * d - c * square), jnp.minimum(c * c * least, 1.0), c * gain))
    return tuple(fresh)


def late_step(state):
    fresh = []
    for x, rest, least, gain in state:
        n = rest.shape[0]
        c = 2.0 / (1.0 + least)
        centred = (1.0 - c) * unit(n) + c * rest
        both = mul_low(jnp.concatenate([centred, x], 0), centred)
        fresh.append((x + both[n:], both[:n], jnp.minimum(c * c * least, 1.0), c * gain))
    return tuple(fresh)


def invert_fast(mats):
    state = []
    lowest = None
    for a in mats:
        back, normal, scale = start(a)
        least = (0.99 * BROADENING**2) * scale
        lowest = least if lowest is None else jnp.minimum(lowest, least)
        state.append((back, normal * scale, least, scale))
    lowest = lowest[0, 0]
    count = jnp.int32(0)
    for value in thresholds():
        count = count + (lowest < value).astype(jnp.int32)
    fixed = FIXED_STEPS[len(mats) - 1]
    for k in range(fixed):
        state = early_step(k, state)
    state = lax.fori_loop(0, jnp.maximum(count - LATE_STEPS - fixed, 0), early_step, tuple(state))
    one = unit(mats[0].shape[0])
    state = tuple((x, one - d, least, gain) for x, d, least, gain in state)
    for _ in range(LATE_STEPS):
        state = late_step(state)
    found, worst = [], jnp.zeros((1, 1), F32)
    for a, (x, _, _, gain) in zip(mats, state):
        x = x * gain
        residue = one - mul_full(a, x)
        worst = jnp.maximum(worst, total(residue * residue))
        found.append(x + mul_split(x, residue))
    return found, worst


def invert_safe(mats):
    n = mats[0].shape[0]
    one = unit(n)
    found = []
    for a in mats:
        back, _, scale = start(a)

        def step(_, x):
            return x + mul_full(x, one - mul_full(a, x))

        x = lax.fori_loop(0, SAFE_STEPS, step, back * scale)
        found.append(x)
    return found, jnp.zeros((1, 1), F32)


def row_form(ref, index=None):
    if index is None:
        return jnp.concatenate([ref[0], ref[1]], 1)
    return jnp.concatenate([ref[index, 0], ref[index, 1]], 1)


def place():
    position = lax.axis_index("space")
    chip = position // 2
    core = position % 2
    right = (chip >= lax.axis_size("space") // 4).astype(jnp.int32)
    outer = (core == right).astype(jnp.int32)
    return position, core, right, outer


def load(pairs, sems):
    copies = [pltpu.make_async_copy(src, dst, sems.at[k]) for k, (src, dst) in enumerate(pairs)]
    for copy in copies:
        copy.start()
    return copies


def prepared(ham, cpl):
    n = ham.shape[-1]
    _, core, _, _ = place()
    energy_count = lax.axis_size("energy")
    rank = lax.axis_index("energy")
    near = rank + 1 - 2 * (rank % 2)
    solved = jnp.where(core == 0, near, (rank + energy_count // 2) % energy_count)
    energy = -2.0 + (solved.astype(F32) + 0.5) * (4.0 / energy_count)
    one = unit(n)
    shift = energy * one + BROADENING * jnp.concatenate([one[:, n:], one[:, :n]], 1)
    hams = [row_form(ham, k) for k in range(2)]
    links = [row_form(cpl, k) for k in range(2)]
    return [shift - 0.5 * (m + adj(m)) for m in hams], links, [adj(m) for m in links]


BACK, CONTACT, LINKS = 4, 8, 10


def block_index(k):
    _, _, right, outer = place()
    return (2 * (1 - outer) if k < 2 else 2 * outer) + (k % 2 + right * (1 - 2 * (k % 2)))


def chip_index(j, core):
    return (2 * core if j < 2 else 2 * (1 - core)) + j % 2


def link_index(k):
    _, core, right, _ = place()
    at = jnp.where(right == 1, chip_index(2 - k, core), chip_index(k, core))
    return at + BACK * right, at + BACK * (1 - right)


def fill(ham, cpl, base, blocks_ref, links_ref):
    blocks, links, backs = prepared(ham, cpl)
    for k in range(2):
        blocks_ref[base + k] = blocks[k]
        links_ref[base + k] = links[k]
        links_ref[BACK + base + k] = backs[k]


def own_kernel(ham_hbm, cpl_hbm, contact_hbm, blocks_ref, links_ref, ham, cpl, contact, sems):
    for copy in load([(ham_hbm, ham), (cpl_hbm, cpl), (contact_hbm, contact)], sems):
        copy.wait()
    fill(ham, cpl, 0, blocks_ref, links_ref)
    lead = row_form(contact)
    links_ref[CONTACT] = lead
    links_ref[CONTACT + 1] = adj(lead)


def join_kernel(own_blocks, own_links, ham, cpl, blocks_ref, links_ref, head_ref):
    _, core, right, _ = place()
    fill(ham, cpl, 2, blocks_ref, links_ref)
    end = chip_index(3, core)
    lead = links_ref[jnp.where(right == 1, BACK + end, CONTACT)]
    lead_back = links_ref[jnp.where(right == 1, end, CONTACT + 1)]
    head_ref[...] = times_half_imag(mul(lead, lead_back))


B0, B1, B2, T0, P1, P2, Q, R, RECORD = range(9)


def chain_links(turned):
    found = [link_index(k) for k in range(3)]
    if turned:
        found = [(b, a) for a, b in found[::-1]]
    return [a for a, _ in found] + [b for _, b in found]


def eliminate(blocks, links, head, record, schur_ref, corner_ref, invert):
    c0, c1, c2, c0h, c1h, c2h = links
    (b0, b2), bad = invert([blocks[0] + head, blocks[2]])
    t0 = mul(b0, c0)
    p1 = mul(b2, c1h)
    p2 = mul(b2, c2)
    record[B0], record[B2], record[T0], record[P1], record[P2] = b0, b2, t0, p1, p2
    middle = blocks[1] - mul(c0h, t0) - mul(c1, p1)
    upper = mul(c1, p2)
    lower = mul(c2h, p1)
    tail = blocks[3] - mul(c2h, p2)
    (b1,), more = invert([middle])
    bad = jnp.maximum(bad, more)
    q = mul(b1, upper)
    r = mul(lower, b1)
    schur = tail - mul(lower, q)
    record[B1], record[Q], record[R] = b1, q, r
    schur_ref[...] = schur
    (corner,), more = invert([schur])
    corner_ref[...] = corner
    return jnp.maximum(bad, more)


def send(links_ref, corner_ref, sender):
    _, core, right, _ = place()
    end = chip_index(3, core)

    @pl.when(right == sender)
    def _():
        corner_ref[...] = mul(mul(links_ref[BACK + end], corner_ref[...]), links_ref[end])


def receive(links_ref, message_ref, sigma_ref, multiplies):
    _, core, right, _ = place()
    end = chip_index(3, core)

    @pl.when(right == multiplies)
    def _():
        sigma_ref[...] = mul(mul(links_ref[end], message_ref[...]), links_ref[BACK + end])

    @pl.when(right != multiplies)
    def _():
        sigma_ref[...] = message_ref[...]


def head_kernel(multiplies, links_ref, message_ref, out_ref):
    receive(links_ref, message_ref, out_ref, multiplies)
    out_ref[...] = -out_ref[...]


def eliminate_kernel(turned, blocks_ref, links_ref, head_ref, record_ref, schur_ref, corner_ref):
    def run(invert):
        bad = eliminate(
            [blocks_ref[block_index(3 - k if turned else k)] for k in range(4)],
            [links_ref[at] for at in chain_links(turned)],
            head_ref[...],
            record_ref,
            schur_ref,
            corner_ref,
            invert,
        )
        send(links_ref, corner_ref, 1 if turned else 0)
        return bad

    bad = jnp.sum(run(invert_fast))

    @pl.when(jnp.logical_not(bad < RESIDUE_LIMIT))
    def _():
        run(invert_safe)


def spread_kernel(links_ref, record_ref, out_ref):
    _, c1, _, c0h, _, c2h = (links_ref[at] for at in chain_links(False))
    b0, b1, b2, t0, p1, p2, q, r = (record_ref[k] for k in range(RECORD))
    w0 = mul(c0h, b0)
    m1 = mul(c1, b2)
    m2 = mul(c2h, b2)
    out_ref[0] = b0 + mul(mul(t0, b1), w0)
    out_ref[1] = b1
    out_ref[2] = b2 + mul(mul(p1, b1), m1)
    out_ref[3] = mul(t0, q)
    out_ref[4] = q
    out_ref[5] = mul(p1, q) + p2
    out_ref[6] = mul(r, w0)
    out_ref[7] = r
    out_ref[8] = mul(r, m1) + m2


def finish_kernel(schur_ref, spread_ref, links_ref, message_ref, mine_ref, theirs_ref, sigma_ref):
    _, _, right, outer = place()
    n = schur_ref.shape[0]
    receive(links_ref, message_ref, sigma_ref, 0)

    def run(invert):
        closed = schur_ref[...] - sigma_ref[...]
        (full,), bad = invert([closed])
        reach = mul_split(jnp.concatenate([spread_ref[3 + j] for j in range(3)], 0), full)
        green = [spread_ref[j] + mul_split(reach[j * n : (j + 1) * n], spread_ref[6 + j]) for j in range(3)] + [full]

        def store(outer_ref, inner_ref):
            for k in range(4):
                ref = outer_ref if k < 2 else inner_ref
                index = jnp.where(right == 1, 1 - k % 2, k % 2)
                ref[index, 0] = green[k][:, :n]
                ref[index, 1] = green[k][:, n:]

        @pl.when(outer == 1)
        def _():
            store(mine_ref, theirs_ref)

        @pl.when(outer == 0)
        def _():
            store(theirs_ref, mine_ref)

        return bad

    bad = jnp.sum(run(invert_fast))

    @pl.when(jnp.logical_not(bad < RESIDUE_LIMIT))
    def _():
        run(invert_safe)


def combine_kernel(
    weight_ref, offset_ref, mine_ref, partner_ref, third_ref, pattern_ref, out_ref
):
    _, core, _, _ = place()
    energy_count = lax.axis_size("energy")
    rank = lax.axis_index("energy")
    half = energy_count // 2
    near = rank + 1 - 2 * (rank % 2)
    away = 2 * rank - near
    far = (rank + half) % energy_count

    def weight_of(source):
        found = jnp.float32(0.0)
        for m in range(weight_ref.shape[0]):
            found = found + jnp.where(offset_ref[m] == rank - source, weight_ref[m], 0.0)
        return found

    near_weight = weight_of(near)
    far_weight = weight_of(far)
    away_weight = weight_of(away)
    mine_weight = jnp.where(core == 0, near_weight, far_weight)
    partner_weight = jnp.where(core == 0, far_weight, near_weight)
    keep = pattern_ref[...].astype(F32)
    for k in range(out_ref.shape[1]):
        for part in range(2):
            value = mine_weight * mine_ref[k, part] + partner_weight * partner_ref[k, part]
            value = value + away_weight * third_ref[k, part]
            out_ref[0, k, part] = value * keep


def kernel(body, shapes, where, scratch=(), aliases=None, result="v"):
    spaces = {"s": pltpu.SMEM, "v": pltpu.VMEM, "a": pl.ANY, "h": pltpu.HBM}
    many = len(shapes) > 1
    if result == "v":
        outs = [pltpu.VMEM(shape, F32) for shape in shapes]
    else:
        outs = [jax.ShapeDtypeStruct(shape, F32) for shape in shapes]
    out_specs = [pl.BlockSpec(memory_space=pltpu.VMEM) for _ in shapes]
    call = pl.pallas_call(
        body,
        out_shape=outs if many else outs[0],
        in_specs=[pl.BlockSpec(memory_space=spaces[w]) for w in where],
        out_specs=out_specs if many else out_specs[0],
        scratch_shapes=list(scratch),
        input_output_aliases=aliases or {},
        compiler_params=pltpu.CompilerParams(vmem_limit_bytes=KERNEL_VMEM),
    )

    def placed(*operands):
        return call(*(
            pltpu.with_memory_space_constraint(x, spaces[w]) if w in "vh" else x for x, w in zip(operands, where)
        ))

    return placed


def on_device(ham_diag, coupling, contact_left, mode_weight, mode_offset, pattern):
    n = ham_diag.shape[-1]
    assert ham_diag.shape[0] == 2
    space = lax.axis_size("space")
    energies = lax.axis_size("energy")
    chips = space // 2
    middle = chips // 2
    assert chips % 2 == 0 and space % 2 == 0 and energies % 4 == 0
    position = lax.axis_index("space")
    chip = position // 2
    depth = jnp.where(chip < middle, chip, chips - 1 - chip)
    swap = [(p, p ^ 1) for p in range(space)]

    row = (n, 2 * n)
    pair = (2, 2, n, n)
    vmem = lambda *shape: pltpu.VMEM(shape, F32)
    sems = lambda count: pltpu.SemaphoreType.DMA((count,))

    ham_far = lax.ppermute(ham_diag, "space", swap)
    cpl_far = lax.ppermute(coupling, "space", swap)

    own = kernel(
        own_kernel, [(4,) + row, (LINKS,) + row], "hhh", [vmem(*pair), vmem(*pair), vmem(2, n, n), sems(3)]
    )(ham_diag, coupling, contact_left)
    blocks, links, head = kernel(
        join_kernel, [(4,) + row, (LINKS,) + row, row], "vvvv", aliases={0: 0, 1: 1}
    )(*own, ham_far, cpl_far)
    forward, backward = (
        kernel(functools.partial(eliminate_kernel, turned), [(RECORD,) + row, row, row], "vvv")
        for turned in (False, True)
    )

    def chip_move(value, pairs):
        return lax.ppermute(value, "space", [(2 * a + k, 2 * b + k) for a, b in pairs for k in range(2)])

    state = forward(blocks, links, head)

    head_inward, head_outward = (
        kernel(functools.partial(head_kernel, multiplies), [row], "vv") for multiplies in (1, 0)
    )
    for d in range(1, middle):
        inward = [(c, c + 1) for c in range(middle - 1)] + [(c + 1, c) for c in range(middle, chips - 1)]
        fresh = forward(blocks, links, head_inward(links, chip_move(state[2], inward)))
        state = [jnp.where(depth >= d, a, b) for a, b in zip(fresh, state)]
    record, schur, corner = state

    message = chip_move(corner, [(middle - 1, middle), (middle, middle - 1)])
    spread = kernel(spread_kernel, [(9,) + row], "vv")(links, record)
    for d in range(middle - 2, -1, -1):
        outward = [(c + 1, c) for c in range(middle - 1)] + [(c, c + 1) for c in range(middle, chips - 1)]
        fresh = backward(blocks, links, head_outward(links, message))
        message = jnp.where(depth == d, chip_move(fresh[2], outward), message)

    mine, theirs = kernel(finish_kernel, [pair, pair], "vvvv", [vmem(*row)])(
        schur, spread, links, message
    )
    ends_from = [(e + 1 - 2 * (1 - e % 2), e) for e in range(energies)]
    wanted = [(source, e) for source, e in ends_from if 0 <= source < energies]
    pairs = []
    for c in range(chips):
        for source, e in wanted:
            for k, site in enumerate((source + 1 - 2 * (source % 2), (source + energies // 2) % energies)):
                pairs.append(((2 * c + k) * energies + site, (2 * c + k) * energies + e))
    third = lax.ppermute(mine, ("space", "energy"), pairs)
    partner = lax.ppermute(theirs, "space", swap)
    return kernel(
        combine_kernel, [(1,) + pair], "ssvvvv", result="a"
    )(mode_weight, mode_offset, mine, partner, third, pattern)


def solution(mesh):
    placed = (P("space", None, None, None), P("space", None, None, None), P(), P(), P(), P())
    return jax.shard_map(
        on_device,
        mesh=mesh,
        in_specs=placed,
        out_specs=P("energy", "space", None, None, None),
        check_vma=False,
    )
```

```python
import functools
import math

import jax
import jax.numpy as jnp
from jax import lax
from jax.experimental import pallas as pl
from jax.experimental.pallas import tpu as pltpu
from jax.sharding import PartitionSpec as P


HIGHEST = lax.Precision.HIGHEST
BROADENING = 0.1
F32 = jnp.float32
BF16 = jnp.bfloat16


FIXED_STEPS = (7, 5)
LATE_STEPS = 2
MOST_STEPS = 20
SETTLED = 0.999
RESIDUE_LIMIT = 4e-3
SAFE_STEPS = 64
KERNEL_VMEM = 24 << 20


def dot(a, b):
    return jnp.dot(a, b, preferred_element_type=F32)


def operand(b):
    n = b.shape[1] // 2
    return jnp.concatenate([b, jnp.concatenate([-b[:, n:], b[:, :n]], 1)], 0)


def halves(a):
    high = a.astype(BF16)
    return high, (a - high.astype(F32)).astype(BF16)


def mul_full(a, b):
    return jnp.dot(a, operand(b), precision=HIGHEST, preferred_element_type=F32)


def mul_split(a, b):
    m = a.shape[0]
    a_high, a_low = halves(a)
    b_high, b_low = halves(b)
    b_high, b_low = operand(b_high), operand(b_low)
    both = dot(jnp.concatenate([a_high, a_low], 0), b_high)
    return both[:m] + (both[m:] + dot(a_high, b_low))


def mul_low(a, b):
    return dot(a.astype(BF16), operand(b.astype(BF16)))


mul = mul_full


def adj(a):
    n = a.shape[1] // 2
    return jnp.concatenate([a[:, :n].T, -a[:, n:].T], 1)


def unit(n):
    row = lax.broadcasted_iota(jnp.int32, (n, 2 * n), 0)
    col = lax.broadcasted_iota(jnp.int32, (n, 2 * n), 1)
    return (row == col).astype(F32)


def times_half_imag(a):
    n = a.shape[1] // 2
    return jnp.concatenate([-0.5 * a[:, n:], 0.5 * a[:, :n]], 1)


def total(a):
    return jnp.sum(jnp.sum(a, axis=0, keepdims=True), axis=1, keepdims=True)


def start(a):
    n = a.shape[0]
    back = adj(a)
    normal = mul_split(a, back)
    size = jnp.sqrt(a[:, :n] * a[:, :n] + a[:, n:] * a[:, n:])
    across = jnp.max(jnp.sum(size, axis=1, keepdims=True), axis=0, keepdims=True)
    down = jnp.max(jnp.sum(size, axis=0, keepdims=True), axis=1, keepdims=True)
    return back, normal, 1.0 / (across * down)


def thresholds():
    value = SETTLED
    for _ in range(MOST_STEPS):
        yield value
        value = value / (2.0 - value + 2.0 * math.sqrt(1.0 - value))


def early_step(_, state):
    fresh = []
    for x, d, least, gain in state:
        c = 2.0 / (1.0 + least)
        square = mul_split(d, d)
        x = 2.0 * x - c * mul_split(x, d)
        fresh.append((x, c * (2.0 * d - c * square), jnp.minimum(c * c * least, 1.0), c * gain))
    return tuple(fresh)


def first_step(state):
    fresh = []
    for x, d, least, gain in state:
        square = mul_split(d, d)
        most = 1.0001 * jnp.sqrt(jnp.sqrt(total(square * square)))
        c = 2.0 / (most + least)
        x = 2.0 * x - c * mul_split(x, d)
        low = c * least
        fresh.append((x, c * (2.0 * d - c * square), jnp.minimum(low * (2.0 - low), 1.0), c * gain))
    return tuple(fresh)


def late_step(state):
    fresh = []
    for x, rest, least, gain in state:
        n = rest.shape[0]
        c = 2.0 / (1.0 + least)
        centred = (1.0 - c) * unit(n) + c * rest
        both = mul_low(jnp.concatenate([centred, x], 0), centred)
        fresh.append((x + both[n:], both[:n], jnp.minimum(c * c * least, 1.0), c * gain))
    return tuple(fresh)


def invert_fast(mats):
    state = []
    for a in mats:
        back, normal, scale = start(a)
        state.append((back, normal * scale, (0.99 * BROADENING**2) * scale, scale))
    state = first_step(state)
    lowest = functools.reduce(jnp.minimum, [least for _, _, least, _ in state])[0, 0]
    count = jnp.int32(0)
    for value in thresholds():
        count = count + (lowest < value).astype(jnp.int32)
    fixed = FIXED_STEPS[len(mats) - 1]
    for k in range(fixed):
        state = early_step(k, state)
    state = lax.fori_loop(0, jnp.maximum(count - LATE_STEPS - fixed, 0), early_step, tuple(state))
    one = unit(mats[0].shape[0])
    state = tuple((x, one - d, least, gain) for x, d, least, gain in state)
    for _ in range(LATE_STEPS):
        state = late_step(state)
    found, worst = [], jnp.zeros((1, 1), F32)
    for a, (x, _, _, gain) in zip(mats, state):
        x = x * gain
        residue = one - mul_full(a, x)
        worst = jnp.maximum(worst, total(residue * residue))
        found.append(x + mul_split(x, residue))
    return found, worst


def invert_safe(mats):
    n = mats[0].shape[0]
    one = unit(n)
    found = []
    for a in mats:
        back, _, scale = start(a)

        def step(_, x):
            return x + mul_full(x, one - mul_full(a, x))

        x = lax.fori_loop(0, SAFE_STEPS, step, back * scale)
        found.append(x)
    return found, jnp.zeros((1, 1), F32)


def row_form(ref, index=None):
    if index is None:
        return jnp.concatenate([ref[0], ref[1]], 1)
    return jnp.concatenate([ref[index, 0], ref[index, 1]], 1)


def place():
    position = lax.axis_index("space")
    chip = position // 2
    core = position % 2
    right = (chip >= lax.axis_size("space") // 4).astype(jnp.int32)
    outer = (core == right).astype(jnp.int32)
    return position, core, right, outer


def load(pairs, sems):
    copies = [pltpu.make_async_copy(src, dst, sems.at[k]) for k, (src, dst) in enumerate(pairs)]
    for copy in copies:
        copy.start()
    return copies


def prepared(ham, cpl):
    n = ham.shape[-1]
    _, core, _, _ = place()
    energy_count = lax.axis_size("energy")
    rank = lax.axis_index("energy")
    near = rank + 1 - 2 * (rank % 2)
    solved = jnp.where(core == 0, near, (rank + energy_count // 2) % energy_count)
    energy = -2.0 + (solved.astype(F32) + 0.5) * (4.0 / energy_count)
    one = unit(n)
    shift = energy * one + BROADENING * jnp.concatenate([one[:, n:], one[:, :n]], 1)
    hams = [row_form(ham, k) for k in range(2)]
    links = [row_form(cpl, k) for k in range(2)]
    return [shift - 0.5 * (m + adj(m)) for m in hams], links, [adj(m) for m in links]


BACK, CONTACT, LINKS = 4, 8, 10


def block_index(k):
    _, _, right, outer = place()
    return (2 * (1 - outer) if k < 2 else 2 * outer) + (k % 2 + right * (1 - 2 * (k % 2)))


def chip_index(j, core):
    return (2 * core if j < 2 else 2 * (1 - core)) + j % 2


def link_index(k):
    _, core, right, _ = place()
    at = jnp.where(right == 1, chip_index(2 - k, core), chip_index(k, core))
    return at + BACK * right, at + BACK * (1 - right)


def fill(ham, cpl, base, blocks_ref, links_ref):
    blocks, links, backs = prepared(ham, cpl)
    for k in range(2):
        blocks_ref[base + k] = blocks[k]
        links_ref[base + k] = links[k]
        links_ref[BACK + base + k] = backs[k]


def own_kernel(ham_hbm, cpl_hbm, contact_hbm, blocks_ref, links_ref, ham, cpl, contact, sems):
    for copy in load([(ham_hbm, ham), (cpl_hbm, cpl), (contact_hbm, contact)], sems):
        copy.wait()
    fill(ham, cpl, 0, blocks_ref, links_ref)
    lead = row_form(contact)
    links_ref[CONTACT] = lead
    links_ref[CONTACT + 1] = adj(lead)


def join_kernel(own_blocks, own_links, ham, cpl, blocks_ref, links_ref, head_ref):
    _, core, right, _ = place()
    fill(ham, cpl, 2, blocks_ref, links_ref)
    end = chip_index(3, core)
    lead = links_ref[jnp.where(right == 1, BACK + end, CONTACT)]
    lead_back = links_ref[jnp.where(right == 1, end, CONTACT + 1)]
    head_ref[...] = times_half_imag(mul(lead, lead_back))


B0, B1, B2, T0, P1, P2, Q, R, RECORD = range(9)


def chain_links(turned):
    found = [link_index(k) for k in range(3)]
    if turned:
        found = [(b, a) for a, b in found[::-1]]
    return [a for a, _ in found] + [b for _, b in found]


def eliminate(blocks, links, head, record, schur_ref, corner_ref, invert):
    c0, c1, c2, c0h, c1h, c2h = links
    (b0, b2), bad = invert([blocks[0] + head, blocks[2]])
    t0 = mul(b0, c0)
    p1 = mul(b2, c1h)
    p2 = mul(b2, c2)
    record[B0], record[B2], record[T0], record[P1], record[P2] = b0, b2, t0, p1, p2
    behind = mul(jnp.concatenate([c1, c2h], 0), p1)
    middle = blocks[1] - mul(c0h, t0) - behind[: c1.shape[0]]
    lower = behind[c1.shape[0] :]
    ahead = mul(jnp.concatenate([c1, c2h], 0), p2)
    upper = ahead[: c1.shape[0]]
    tail = blocks[3] - ahead[c1.shape[0] :]
    (b1,), more = invert([middle])
    bad = jnp.maximum(bad, more)
    q = mul(b1, upper)
    r = mul(lower, b1)
    schur = tail - mul(lower, q)
    record[B1], record[Q], record[R] = b1, q, r
    schur_ref[...] = schur
    (corner,), more = invert([schur])
    corner_ref[...] = corner
    return jnp.maximum(bad, more)


def send(links_ref, corner_ref, sender):
    _, core, right, _ = place()
    end = chip_index(3, core)

    @pl.when(right == sender)
    def _():
        corner_ref[...] = mul(mul(links_ref[BACK + end], corner_ref[...]), links_ref[end])


def receive(links_ref, message_ref, sigma_ref, multiplies):
    _, core, right, _ = place()
    end = chip_index(3, core)

    @pl.when(right == multiplies)
    def _():
        sigma_ref[...] = mul(mul(links_ref[end], message_ref[...]), links_ref[BACK + end])

    @pl.when(right != multiplies)
    def _():
        sigma_ref[...] = message_ref[...]


def head_kernel(multiplies, links_ref, message_ref, out_ref):
    receive(links_ref, message_ref, out_ref, multiplies)
    out_ref[...] = -out_ref[...]


def eliminate_kernel(turned, blocks_ref, links_ref, head_ref, record_ref, schur_ref, corner_ref):
    def run(invert):
        bad = eliminate(
            [blocks_ref[block_index(3 - k if turned else k)] for k in range(4)],
            [links_ref[at] for at in chain_links(turned)],
            head_ref[...],
            record_ref,
            schur_ref,
            corner_ref,
            invert,
        )
        send(links_ref, corner_ref, 1 if turned else 0)
        return bad

    bad = jnp.sum(run(invert_fast))

    @pl.when(jnp.logical_not(bad < RESIDUE_LIMIT))
    def _():
        run(invert_safe)


def spread_kernel(links_ref, record_ref, out_ref):
    _, c1, _, c0h, _, c2h = (links_ref[at] for at in chain_links(False))
    b0, b1, b2, t0, p1, p2, q, r = (record_ref[k] for k in range(RECORD))
    w0 = mul(c0h, b0)
    m1 = mul(c1, b2)
    m2 = mul(c2h, b2)
    out_ref[0] = b0 + mul(mul(t0, b1), w0)
    out_ref[1] = b1
    out_ref[2] = b2 + mul(mul(p1, b1), m1)
    out_ref[3] = mul(t0, q)
    out_ref[4] = q
    out_ref[5] = mul(p1, q) + p2
    out_ref[6] = mul(r, w0)
    out_ref[7] = r
    out_ref[8] = mul(r, m1) + m2


def finish_kernel(schur_ref, spread_ref, links_ref, message_ref, mine_ref, theirs_ref, sigma_ref):
    _, _, right, outer = place()
    n = schur_ref.shape[0]
    receive(links_ref, message_ref, sigma_ref, 0)

    def run(invert):
        closed = schur_ref[...] - sigma_ref[...]
        (full,), bad = invert([closed])
        reach = mul_split(jnp.concatenate([spread_ref[3 + j] for j in range(3)], 0), full)
        green = [spread_ref[j] + mul_split(reach[j * n : (j + 1) * n], spread_ref[6 + j]) for j in range(3)] + [full]

        def store(outer_ref, inner_ref):
            for k in range(4):
                ref = outer_ref if k < 2 else inner_ref
                index = jnp.where(right == 1, 1 - k % 2, k % 2)
                ref[index, 0] = green[k][:, :n]
                ref[index, 1] = green[k][:, n:]

        @pl.when(outer == 1)
        def _():
            store(mine_ref, theirs_ref)

        @pl.when(outer == 0)
        def _():
            store(theirs_ref, mine_ref)

        return bad

    bad = jnp.sum(run(invert_fast))

    @pl.when(jnp.logical_not(bad < RESIDUE_LIMIT))
    def _():
        run(invert_safe)


def combine_kernel(
    weight_ref, offset_ref, mine_ref, partner_ref, third_ref, pattern_ref, out_ref
):
    _, core, _, _ = place()
    energy_count = lax.axis_size("energy")
    rank = lax.axis_index("energy")
    half = energy_count // 2
    near = rank + 1 - 2 * (rank % 2)
    away = 2 * rank - near
    far = (rank + half) % energy_count

    def weight_of(source):
        found = jnp.float32(0.0)
        for m in range(weight_ref.shape[0]):
            found = found + jnp.where(offset_ref[m] == rank - source, weight_ref[m], 0.0)
        return found

    near_weight = weight_of(near)
    far_weight = weight_of(far)
    away_weight = weight_of(away)
    mine_weight = jnp.where(core == 0, near_weight, far_weight)
    partner_weight = jnp.where(core == 0, far_weight, near_weight)
    keep = pattern_ref[...].astype(F32)
    for k in range(out_ref.shape[1]):
        for part in range(2):
            value = mine_weight * mine_ref[k, part] + partner_weight * partner_ref[k, part]
            value = value + away_weight * third_ref[k, part]
            out_ref[0, k, part] = value * keep


def kernel(body, shapes, where, scratch=(), aliases=None, result="v"):
    spaces = {"s": pltpu.SMEM, "v": pltpu.VMEM, "a": pl.ANY, "h": pltpu.HBM}
    many = len(shapes) > 1
    if result == "v":
        outs = [pltpu.VMEM(shape, F32) for shape in shapes]
    else:
        outs = [jax.ShapeDtypeStruct(shape, F32) for shape in shapes]
    out_specs = [pl.BlockSpec(memory_space=pltpu.VMEM) for _ in shapes]
    call = pl.pallas_call(
        body,
        out_shape=outs if many else outs[0],
        in_specs=[pl.BlockSpec(memory_space=spaces[w]) for w in where],
        out_specs=out_specs if many else out_specs[0],
        scratch_shapes=list(scratch),
        input_output_aliases=aliases or {},
        compiler_params=pltpu.CompilerParams(vmem_limit_bytes=KERNEL_VMEM),
    )

    def placed(*operands):
        return call(*(
            pltpu.with_memory_space_constraint(x, spaces[w]) if w in "vh" else x for x, w in zip(operands, where)
        ))

    return placed


def on_device(ham_diag, coupling, contact_left, mode_weight, mode_offset, pattern):
    n = ham_diag.shape[-1]
    assert ham_diag.shape[0] == 2
    space = lax.axis_size("space")
    energies = lax.axis_size("energy")
    chips = space // 2
    middle = chips // 2
    assert chips % 2 == 0 and space % 2 == 0 and energies % 4 == 0
    position = lax.axis_index("space")
    chip = position // 2
    depth = jnp.where(chip < middle, chip, chips - 1 - chip)
    swap = [(p, p ^ 1) for p in range(space)]

    row = (n, 2 * n)
    pair = (2, 2, n, n)
    vmem = lambda *shape: pltpu.VMEM(shape, F32)
    sems = lambda count: pltpu.SemaphoreType.DMA((count,))

    ham_far = lax.ppermute(ham_diag, "space", swap)
    cpl_far = lax.ppermute(coupling, "space", swap)

    own = kernel(
        own_kernel, [(4,) + row, (LINKS,) + row], "hhh", [vmem(*pair), vmem(*pair), vmem(2, n, n), sems(3)]
    )(ham_diag, coupling, contact_left)
    blocks, links, head = kernel(
        join_kernel, [(4,) + row, (LINKS,) + row, row], "vvvv", aliases={0: 0, 1: 1}
    )(*own, ham_far, cpl_far)
    forward, backward = (
        kernel(functools.partial(eliminate_kernel, turned), [(RECORD,) + row, row, row], "vvv")
        for turned in (False, True)
    )

    def chip_move(value, pairs):
        return lax.ppermute(value, "space", [(2 * a + k, 2 * b + k) for a, b in pairs for k in range(2)])

    state = forward(blocks, links, head)

    head_inward, head_outward = (
        kernel(functools.partial(head_kernel, multiplies), [row], "vv") for multiplies in (1, 0)
    )
    for d in range(1, middle):
        inward = [(c, c + 1) for c in range(middle - 1)] + [(c + 1, c) for c in range(middle, chips - 1)]
        fresh = forward(blocks, links, head_inward(links, chip_move(state[2], inward)))
        state = [jnp.where(depth >= d, a, b) for a, b in zip(fresh, state)]
    record, schur, corner = state

    message = chip_move(corner, [(middle - 1, middle), (middle, middle - 1)])
    spread = kernel(spread_kernel, [(9,) + row], "vv")(links, record)
    for d in range(middle - 2, -1, -1):
        outward = [(c + 1, c) for c in range(middle - 1)] + [(c, c + 1) for c in range(middle, chips - 1)]
        fresh = backward(blocks, links, head_outward(links, message))
        message = jnp.where(depth == d, chip_move(fresh[2], outward), message)

    mine, theirs = kernel(finish_kernel, [pair, pair], "vvvv", [vmem(*row)])(
        schur, spread, links, message
    )
    ends_from = [(e + 1 - 2 * (1 - e % 2), e) for e in range(energies)]
    wanted = [(source, e) for source, e in ends_from if 0 <= source < energies]
    pairs = []
    for c in range(chips):
        for source, e in wanted:
            for k, site in enumerate((source + 1 - 2 * (source % 2), (source + energies // 2) % energies)):
                pairs.append(((2 * c + k) * energies + site, (2 * c + k) * energies + e))
    third = lax.ppermute(mine, ("space", "energy"), pairs)
    partner = lax.ppermute(theirs, "space", swap)
    return kernel(
        combine_kernel, [(1,) + pair], "ssvvvv", result="a"
    )(mode_weight, mode_offset, mine, partner, third, pattern)


def solution(mesh):
    placed = (P("space", None, None, None), P("space", None, None, None), P(), P(), P(), P())
    return jax.shard_map(
        on_device,
        mesh=mesh,
        in_specs=placed,
        out_specs=P("energy", "space", None, None, None),
        check_vma=False,
    )
```

```python
import functools
import math

import jax
import jax.numpy as jnp
from jax import lax
from jax.experimental import pallas as pl
from jax.experimental.pallas import tpu as pltpu
from jax.sharding import PartitionSpec as P


HIGHEST = lax.Precision.HIGHEST
BROADENING = 0.1
F32 = jnp.float32
BF16 = jnp.bfloat16


FIXED_STEPS = (7, 5)
LATE_STEPS = 2
MOST_STEPS = 20
SETTLED = 0.996
RESIDUE_LIMIT = 4e-3
SAFE_STEPS = 64
KERNEL_VMEM = 24 << 20


def dot(a, b):
    return jnp.dot(a, b, preferred_element_type=F32)


def operand(b):
    n = b.shape[1] // 2
    return jnp.concatenate([b, jnp.concatenate([-b[:, n:], b[:, :n]], 1)], 0)


def halves(a):
    high = a.astype(BF16)
    return high, (a - high.astype(F32)).astype(BF16)


def mul_full(a, b):
    return jnp.dot(a, operand(b), precision=HIGHEST, preferred_element_type=F32)


def mul_split(a, b):
    m = a.shape[0]
    a_high, a_low = halves(a)
    b_high, b_low = halves(b)
    b_high, b_low = operand(b_high), operand(b_low)
    both = dot(jnp.concatenate([a_high, a_low], 0), b_high)
    return both[:m] + (both[m:] + dot(a_high, b_low))


def mul_low(a, b):
    return dot(a.astype(BF16), operand(b.astype(BF16)))


mul = mul_full


def adj(a):
    n = a.shape[1] // 2
    return jnp.concatenate([a[:, :n].T, -a[:, n:].T], 1)


def unit(n):
    row = lax.broadcasted_iota(jnp.int32, (n, 2 * n), 0)
    col = lax.broadcasted_iota(jnp.int32, (n, 2 * n), 1)
    return (row == col).astype(F32)


def times_half_imag(a):
    n = a.shape[1] // 2
    return jnp.concatenate([-0.5 * a[:, n:], 0.5 * a[:, :n]], 1)


def total(a):
    return jnp.sum(jnp.sum(a, axis=0, keepdims=True), axis=1, keepdims=True)


def start(a):
    n = a.shape[0]
    back = adj(a)
    normal = mul_split(a, back)
    size = jnp.sqrt(a[:, :n] * a[:, :n] + a[:, n:] * a[:, n:])
    across = jnp.max(jnp.sum(size, axis=1, keepdims=True), axis=0, keepdims=True)
    down = jnp.max(jnp.sum(size, axis=0, keepdims=True), axis=1, keepdims=True)
    return back, normal, 1.0 / (across * down)


def thresholds():
    value = SETTLED
    for _ in range(MOST_STEPS):
        yield value
        value = value / (2.0 - value + 2.0 * math.sqrt(1.0 - value))


def early_step(_, state):
    fresh = []
    for x, d, least, gain in state:
        c = 2.0 / (1.0 + least)
        square = mul_split(d, d)
        x = 2.0 * x - c * mul_split(x, d)
        fresh.append((x, c * (2.0 * d - c * square), jnp.minimum(c * c * least, 1.0), c * gain))
    return tuple(fresh)


def first_step(state):
    fresh = []
    for x, d, least, gain in state:
        square = mul_split(d, d)
        most = 1.0001 * jnp.sqrt(jnp.sqrt(total(square * square)))
        c = 2.0 / (most + least)
        x = 2.0 * x - c * mul_split(x, d)
        low = c * least
        fresh.append((x, c * (2.0 * d - c * square), jnp.minimum(low * (2.0 - low), 1.0), c * gain))
    return tuple(fresh)


def late_step(state):
    fresh = []
    for x, rest, least, gain in state:
        n = rest.shape[0]
        c = 2.0 / (1.0 + least)
        centred = (1.0 - c) * unit(n) + c * rest
        both = mul_low(jnp.concatenate([centred, x], 0), centred)
        fresh.append((x + both[n:], both[:n], jnp.minimum(c * c * least, 1.0), c * gain))
    return tuple(fresh)


def invert_fast(mats):
    state = []
    for a in mats:
        back, normal, scale = start(a)
        state.append((back, normal * scale, (0.99 * BROADENING**2) * scale, scale))
    state = first_step(state)
    lowest = functools.reduce(jnp.minimum, [least for _, _, least, _ in state])[0, 0]
    count = jnp.int32(0)
    for value in thresholds():
        count = count + (lowest < value).astype(jnp.int32)
    fixed = FIXED_STEPS[len(mats) - 1]
    for k in range(fixed):
        state = early_step(k, state)
    state = lax.fori_loop(0, jnp.maximum(count - LATE_STEPS - fixed, 0), early_step, tuple(state))
    one = unit(mats[0].shape[0])
    state = tuple((x, one - d, least, gain) for x, d, least, gain in state)
    for _ in range(LATE_STEPS):
        state = late_step(state)
    found, worst = [], jnp.zeros((1, 1), F32)
    for a, (x, _, _, gain) in zip(mats, state):
        x = x * gain
        residue = one - mul_full(a, x)
        worst = jnp.maximum(worst, total(residue * residue))
        found.append(x + mul_split(x, residue))
    return found, worst


def invert_safe(mats):
    n = mats[0].shape[0]
    one = unit(n)
    found = []
    for a in mats:
        back, _, scale = start(a)

        def step(_, x):
            return x + mul_full(x, one - mul_full(a, x))

        x = lax.fori_loop(0, SAFE_STEPS, step, back * scale)
        found.append(x)
    return found, jnp.zeros((1, 1), F32)


def row_form(ref, index=None):
    if index is None:
        return jnp.concatenate([ref[0], ref[1]], 1)
    return jnp.concatenate([ref[index, 0], ref[index, 1]], 1)


def place():
    position = lax.axis_index("space")
    chip = position // 2
    core = position % 2
    right = (chip >= lax.axis_size("space") // 4).astype(jnp.int32)
    outer = (core == right).astype(jnp.int32)
    return position, core, right, outer


def load(pairs, sems):
    copies = [pltpu.make_async_copy(src, dst, sems.at[k]) for k, (src, dst) in enumerate(pairs)]
    for copy in copies:
        copy.start()
    return copies


def prepared(ham, cpl):
    n = ham.shape[-1]
    _, core, _, _ = place()
    energy_count = lax.axis_size("energy")
    rank = lax.axis_index("energy")
    near = rank + 1 - 2 * (rank % 2)
    solved = jnp.where(core == 0, near, (rank + energy_count // 2) % energy_count)
    energy = -2.0 + (solved.astype(F32) + 0.5) * (4.0 / energy_count)
    one = unit(n)
    shift = energy * one + BROADENING * jnp.concatenate([one[:, n:], one[:, :n]], 1)
    hams = [row_form(ham, k) for k in range(2)]
    links = [row_form(cpl, k) for k in range(2)]
    return [shift - 0.5 * (m + adj(m)) for m in hams], links, [adj(m) for m in links]


BACK, CONTACT, LINKS = 4, 8, 10


def block_index(k):
    _, _, right, outer = place()
    return (2 * (1 - outer) if k < 2 else 2 * outer) + (k % 2 + right * (1 - 2 * (k % 2)))


def chip_index(j, core):
    return (2 * core if j < 2 else 2 * (1 - core)) + j % 2


def link_index(k):
    _, core, right, _ = place()
    at = jnp.where(right == 1, chip_index(2 - k, core), chip_index(k, core))
    return at + BACK * right, at + BACK * (1 - right)


def fill(ham, cpl, base, blocks_ref, links_ref):
    blocks, links, backs = prepared(ham, cpl)
    for k in range(2):
        blocks_ref[base + k] = blocks[k]
        links_ref[base + k] = links[k]
        links_ref[BACK + base + k] = backs[k]


def own_kernel(ham_hbm, cpl_hbm, contact_hbm, blocks_ref, links_ref, ham, cpl, contact, sems):
    for copy in load([(ham_hbm, ham), (cpl_hbm, cpl), (contact_hbm, contact)], sems):
        copy.wait()
    fill(ham, cpl, 0, blocks_ref, links_ref)
    lead = row_form(contact)
    links_ref[CONTACT] = lead
    links_ref[CONTACT + 1] = adj(lead)


def join_kernel(own_blocks, own_links, ham, cpl, blocks_ref, links_ref, head_ref):
    _, core, right, _ = place()
    fill(ham, cpl, 2, blocks_ref, links_ref)
    end = chip_index(3, core)
    lead = links_ref[jnp.where(right == 1, BACK + end, CONTACT)]
    lead_back = links_ref[jnp.where(right == 1, end, CONTACT + 1)]
    head_ref[...] = times_half_imag(mul(lead, lead_back))


B0, B1, B2, T0, P1, P2, Q, R, RECORD = range(9)


def chain_links(turned):
    found = [link_index(k) for k in range(3)]
    if turned:
        found = [(b, a) for a, b in found[::-1]]
    return [a for a, _ in found] + [b for _, b in found]


def eliminate(blocks, links, head, record, schur_ref, corner_ref, invert):
    c0, c1, c2, c0h, c1h, c2h = links
    (b0, b2), bad = invert([blocks[0] + head, blocks[2]])
    t0 = mul(b0, c0)
    p1 = mul(b2, c1h)
    p2 = mul(b2, c2)
    record[B0], record[B2], record[T0], record[P1], record[P2] = b0, b2, t0, p1, p2
    behind = mul(jnp.concatenate([c1, c2h], 0), p1)
    middle = blocks[1] - mul(c0h, t0) - behind[: c1.shape[0]]
    lower = behind[c1.shape[0] :]
    ahead = mul(jnp.concatenate([c1, c2h], 0), p2)
    upper = ahead[: c1.shape[0]]
    tail = blocks[3] - ahead[c1.shape[0] :]
    (b1,), more = invert([middle])
    bad = jnp.maximum(bad, more)
    q = mul(b1, upper)
    r = mul(lower, b1)
    schur = tail - mul(lower, q)
    record[B1], record[Q], record[R] = b1, q, r
    schur_ref[...] = schur
    (corner,), more = invert([schur])
    corner_ref[...] = corner
    return jnp.maximum(bad, more)


def send(links_ref, corner_ref, sender):
    _, core, right, _ = place()
    end = chip_index(3, core)

    @pl.when(right == sender)
    def _():
        corner_ref[...] = mul(mul(links_ref[BACK + end], corner_ref[...]), links_ref[end])


def receive(links_ref, message_ref, sigma_ref, multiplies):
    _, core, right, _ = place()
    end = chip_index(3, core)

    @pl.when(right == multiplies)
    def _():
        sigma_ref[...] = mul(mul(links_ref[end], message_ref[...]), links_ref[BACK + end])

    @pl.when(right != multiplies)
    def _():
        sigma_ref[...] = message_ref[...]


def head_kernel(multiplies, links_ref, message_ref, out_ref):
    receive(links_ref, message_ref, out_ref, multiplies)
    out_ref[...] = -out_ref[...]


def eliminate_kernel(turned, blocks_ref, links_ref, head_ref, record_ref, schur_ref, corner_ref):
    def run(invert):
        bad = eliminate(
            [blocks_ref[block_index(3 - k if turned else k)] for k in range(4)],
            [links_ref[at] for at in chain_links(turned)],
            head_ref[...],
            record_ref,
            schur_ref,
            corner_ref,
            invert,
        )
        send(links_ref, corner_ref, 1 if turned else 0)
        return bad

    bad = jnp.sum(run(invert_fast))

    @pl.when(jnp.logical_not(bad < RESIDUE_LIMIT))
    def _():
        run(invert_safe)


def spread_kernel(weight_ref, offset_ref, links_ref, record_ref, out_ref, weights_ref):
    for k, value in enumerate(weights(weight_ref, offset_ref)):
        weights_ref[k] = jnp.full(weights_ref.shape[1:], value, F32)
    _, c1, _, c0h, _, c2h = (links_ref[at] for at in chain_links(False))
    b0, b1, b2, t0, p1, p2, q, r = (record_ref[k] for k in range(RECORD))
    w0 = mul(c0h, b0)
    m1 = mul(c1, b2)
    m2 = mul(c2h, b2)
    out_ref[0] = b0 + mul(mul(t0, b1), w0)
    out_ref[1] = b1
    out_ref[2] = b2 + mul(mul(p1, b1), m1)
    out_ref[3] = mul(t0, q)
    out_ref[4] = q
    out_ref[5] = mul(p1, q) + p2
    out_ref[6] = mul(r, w0)
    out_ref[7] = r
    out_ref[8] = mul(r, m1) + m2


def finish_kernel(schur_ref, spread_ref, links_ref, message_ref, mine_ref, theirs_ref, sigma_ref):
    _, _, right, outer = place()
    n = schur_ref.shape[0]
    receive(links_ref, message_ref, sigma_ref, 0)

    def run(invert):
        closed = schur_ref[...] - sigma_ref[...]
        (full,), bad = invert([closed])
        reach = mul_split(jnp.concatenate([spread_ref[3 + j] for j in range(3)], 0), full)
        green = [spread_ref[j] + mul_split(reach[j * n : (j + 1) * n], spread_ref[6 + j]) for j in range(3)] + [full]

        def store(outer_ref, inner_ref):
            for k in range(4):
                ref = outer_ref if k < 2 else inner_ref
                index = jnp.where(right == 1, 1 - k % 2, k % 2)
                ref[index, 0] = green[k][:, :n]
                ref[index, 1] = green[k][:, n:]

        @pl.when(outer == 1)
        def _():
            store(mine_ref, theirs_ref)

        @pl.when(outer == 0)
        def _():
            store(theirs_ref, mine_ref)

        return bad

    bad = jnp.sum(run(invert_fast))

    @pl.when(jnp.logical_not(bad < RESIDUE_LIMIT))
    def _():
        run(invert_safe)


def weights(weight_ref, offset_ref):
    _, core, _, _ = place()
    energy_count = lax.axis_size("energy")
    rank = lax.axis_index("energy")
    near = rank + 1 - 2 * (rank % 2)

    def weight_of(source):
        found = jnp.float32(0.0)
        for m in range(weight_ref.shape[0]):
            found = found + jnp.where(offset_ref[m] == rank - source, weight_ref[m], 0.0)
        return found

    near_weight = weight_of(near)
    far_weight = weight_of((rank + energy_count // 2) % energy_count)
    mine = jnp.where(core == 0, near_weight, far_weight)
    partner = jnp.where(core == 0, far_weight, near_weight)
    return mine, partner, weight_of(2 * rank - near)


def combine_kernel(weights_ref, mine_ref, partner_ref, third_ref, pattern_ref, out_ref):
    mine, partner, away = (weights_ref[k, 0:1, :] for k in range(3))
    keep = pattern_ref[...].astype(F32)
    for k in range(out_ref.shape[1]):
        for part in range(2):
            value = mine * mine_ref[k, part] + partner * partner_ref[k, part]
            out_ref[0, k, part] = (value + away * third_ref[k, part]) * keep


def kernel(body, shapes, where, scratch=(), aliases=None, result="v"):
    spaces = {"s": pltpu.SMEM, "v": pltpu.VMEM, "a": pl.ANY, "h": pltpu.HBM}
    many = len(shapes) > 1
    if result == "v":
        outs = [pltpu.VMEM(shape, F32) for shape in shapes]
    else:
        outs = [jax.ShapeDtypeStruct(shape, F32) for shape in shapes]
    out_specs = [pl.BlockSpec(memory_space=pltpu.VMEM) for _ in shapes]
    call = pl.pallas_call(
        body,
        out_shape=outs if many else outs[0],
        in_specs=[pl.BlockSpec(memory_space=spaces[w]) for w in where],
        out_specs=out_specs if many else out_specs[0],
        scratch_shapes=list(scratch),
        input_output_aliases=aliases or {},
        compiler_params=pltpu.CompilerParams(vmem_limit_bytes=KERNEL_VMEM),
    )

    def placed(*operands):
        return call(*(
            pltpu.with_memory_space_constraint(x, spaces[w]) if w in "vh" else x for x, w in zip(operands, where)
        ))

    return placed


def on_device(ham_diag, coupling, contact_left, mode_weight, mode_offset, pattern):
    n = ham_diag.shape[-1]
    assert ham_diag.shape[0] == 2
    space = lax.axis_size("space")
    energies = lax.axis_size("energy")
    chips = space // 2
    middle = chips // 2
    assert chips % 2 == 0 and space % 2 == 0 and energies % 4 == 0
    position = lax.axis_index("space")
    chip = position // 2
    depth = jnp.where(chip < middle, chip, chips - 1 - chip)
    swap = [(p, p ^ 1) for p in range(space)]

    row = (n, 2 * n)
    pair = (2, 2, n, n)
    vmem = lambda *shape: pltpu.VMEM(shape, F32)
    sems = lambda count: pltpu.SemaphoreType.DMA((count,))

    ham_far = lax.ppermute(ham_diag, "space", swap)
    cpl_far = lax.ppermute(coupling, "space", swap)

    own = kernel(
        own_kernel, [(4,) + row, (LINKS,) + row], "hhh", [vmem(*pair), vmem(*pair), vmem(2, n, n), sems(3)]
    )(ham_diag, coupling, contact_left)
    blocks, links, head = kernel(
        join_kernel, [(4,) + row, (LINKS,) + row, row], "vvvv", aliases={0: 0, 1: 1}
    )(*own, ham_far, cpl_far)
    forward, backward = (
        kernel(functools.partial(eliminate_kernel, turned), [(RECORD,) + row, row, row], "vvv")
        for turned in (False, True)
    )

    def chip_move(value, pairs):
        return lax.ppermute(value, "space", [(2 * a + k, 2 * b + k) for a, b in pairs for k in range(2)])

    state = forward(blocks, links, head)

    head_inward, head_outward = (
        kernel(functools.partial(head_kernel, multiplies), [row], "vv") for multiplies in (1, 0)
    )
    for d in range(1, middle):
        inward = [(c, c + 1) for c in range(middle - 1)] + [(c + 1, c) for c in range(middle, chips - 1)]
        fresh = forward(blocks, links, head_inward(links, chip_move(state[2], inward)))
        state = [jnp.where(depth >= d, a, b) for a, b in zip(fresh, state)]
    record, schur, corner = state

    message = chip_move(corner, [(middle - 1, middle), (middle, middle - 1)])
    spread, shares = kernel(spread_kernel, [(9,) + row, (3, 8, n)], "ssvv")(
        mode_weight, mode_offset, links, record
    )
    for d in range(middle - 2, -1, -1):
        outward = [(c + 1, c) for c in range(middle - 1)] + [(c, c + 1) for c in range(middle, chips - 1)]
        fresh = backward(blocks, links, head_outward(links, message))
        message = jnp.where(depth == d, chip_move(fresh[2], outward), message)

    mine, theirs = kernel(finish_kernel, [pair, pair], "vvvv", [vmem(*row)])(
        schur, spread, links, message
    )
    ends_from = [(e + 1 - 2 * (1 - e % 2), e) for e in range(energies)]
    wanted = [(source, e) for source, e in ends_from if 0 <= source < energies]
    pairs = []
    for c in range(chips):
        for source, e in wanted:
            for k, site in enumerate((source + 1 - 2 * (source % 2), (source + energies // 2) % energies)):
                pairs.append(((2 * c + k) * energies + site, (2 * c + k) * energies + e))
    third = lax.ppermute(mine, ("space", "energy"), pairs)
    partner = lax.ppermute(theirs, "space", swap)
    return kernel(combine_kernel, [(1,) + pair], "vvvvv", result="a")(shares, mine, partner, third, pattern)


def solution(mesh):
    placed = (P("space", None, None, None), P("space", None, None, None), P(), P(), P(), P())
    return jax.shard_map(
        on_device,
        mesh=mesh,
        in_specs=placed,
        out_specs=P("energy", "space", None, None, None),
        check_vma=False,
    )
```

```python
import functools
import math

import jax
import jax.numpy as jnp
from jax import lax
from jax.experimental import pallas as pl
from jax.experimental.pallas import tpu as pltpu
from jax.sharding import PartitionSpec as P


HIGHEST = lax.Precision.HIGHEST
BROADENING = 0.1
F32 = jnp.float32
BF16 = jnp.bfloat16


FIXED_STEPS = (7, 5)
LATE_STEPS = 2
MOST_STEPS = 20
SETTLED = 0.996
RESIDUE_LIMIT = 4e-3
SAFE_STEPS = 64
KERNEL_VMEM = 24 << 20


def dot(a, b):
    return jnp.dot(a, b, preferred_element_type=F32)


def operand(b):
    n = b.shape[1] // 2
    return jnp.concatenate([b, jnp.concatenate([-b[:, n:], b[:, :n]], 1)], 0)


def halves(a):
    high = a.astype(BF16)
    return high, (a - high.astype(F32)).astype(BF16)


def mul_full(a, b):
    return jnp.dot(a, operand(b), precision=HIGHEST, preferred_element_type=F32)


def mul_split(a, b):
    m = a.shape[0]
    a_high, a_low = halves(a)
    b_high, b_low = halves(b)
    b_high, b_low = operand(b_high), operand(b_low)
    both = dot(jnp.concatenate([a_high, a_low], 0), b_high)
    return both[:m] + (both[m:] + dot(a_high, b_low))


def mul_low(a, b):
    return dot(a.astype(BF16), operand(b.astype(BF16)))


mul = mul_full


def adj(a):
    n = a.shape[1] // 2
    return jnp.concatenate([a[:, :n].T, -a[:, n:].T], 1)


def unit(n):
    row = lax.broadcasted_iota(jnp.int32, (n, 2 * n), 0)
    col = lax.broadcasted_iota(jnp.int32, (n, 2 * n), 1)
    return (row == col).astype(F32)


def times_half_imag(a):
    n = a.shape[1] // 2
    return jnp.concatenate([-0.5 * a[:, n:], 0.5 * a[:, :n]], 1)


def total(a):
    return jnp.sum(jnp.sum(a, axis=0, keepdims=True), axis=1, keepdims=True)


def start(a):
    n = a.shape[0]
    back = adj(a)
    normal = mul_split(a, back)
    size = jnp.sqrt(a[:, :n] * a[:, :n] + a[:, n:] * a[:, n:])
    across = jnp.max(jnp.sum(size, axis=1, keepdims=True), axis=0, keepdims=True)
    down = jnp.max(jnp.sum(size, axis=0, keepdims=True), axis=1, keepdims=True)
    return back, normal, 1.0 / (across * down)


def thresholds():
    value = SETTLED
    for _ in range(MOST_STEPS):
        yield value
        value = value / (2.0 - value + 2.0 * math.sqrt(1.0 - value))


def early_step(_, state):
    fresh = []
    for x, d, least, gain in state:
        c = 2.0 / (1.0 + least)
        square = mul_split(d, d)
        x = 2.0 * x - c * mul_split(x, d)
        fresh.append((x, c * (2.0 * d - c * square), jnp.minimum(c * c * least, 1.0), c * gain))
    return tuple(fresh)


def first_step(state):
    fresh = []
    for x, d, least, gain in state:
        square = mul_split(d, d)
        most = 1.0001 * jnp.sqrt(jnp.sqrt(total(square * square)))
        c = 2.0 / (most + least)
        x = 2.0 * x - c * mul_split(x, d)
        low = c * least
        fresh.append((x, c * (2.0 * d - c * square), jnp.minimum(low * (2.0 - low), 1.0), c * gain))
    return tuple(fresh)


def late_step(state):
    fresh = []
    for x, rest, least, gain in state:
        n = rest.shape[0]
        c = 2.0 / (1.0 + least)
        centred = (1.0 - c) * unit(n) + c * rest
        square = mul_low(centred, centred)
        fresh.append((x + mul_low(x, centred), square, jnp.minimum(c * c * least, 1.0), c * gain))
    return tuple(fresh)


def invert_fast(mats):
    state = []
    for a in mats:
        back, normal, scale = start(a)
        state.append((back, normal * scale, (0.99 * BROADENING**2) * scale, scale))
    state = first_step(state)
    lowest = functools.reduce(jnp.minimum, [least for _, _, least, _ in state])[0, 0]
    count = jnp.int32(0)
    for value in thresholds():
        count = count + (lowest < value).astype(jnp.int32)
    fixed = FIXED_STEPS[len(mats) - 1]
    for k in range(fixed):
        state = early_step(k, state)
    state = lax.fori_loop(0, jnp.maximum(count - LATE_STEPS - fixed, 0), early_step, tuple(state))
    one = unit(mats[0].shape[0])
    state = tuple((x, one - d, least, gain) for x, d, least, gain in state)
    for _ in range(LATE_STEPS):
        state = late_step(state)
    found, worst = [], jnp.zeros((1, 1), F32)
    for a, (x, _, _, gain) in zip(mats, state):
        x = x * gain
        residue = one - mul_full(a, x)
        worst = jnp.maximum(worst, total(residue * residue))
        found.append(x + mul_split(x, residue))
    return found, worst


def invert_safe(mats):
    n = mats[0].shape[0]
    one = unit(n)
    found = []
    for a in mats:
        back, _, scale = start(a)

        def step(_, x):
            return x + mul_full(x, one - mul_full(a, x))

        x = lax.fori_loop(0, SAFE_STEPS, step, back * scale)
        found.append(x)
    return found, jnp.zeros((1, 1), F32)


def row_form(ref, index=None):
    if index is None:
        return jnp.concatenate([ref[0], ref[1]], 1)
    return jnp.concatenate([ref[index, 0], ref[index, 1]], 1)


def place():
    position = lax.axis_index("space")
    chip = position // 2
    core = position % 2
    right = (chip >= lax.axis_size("space") // 4).astype(jnp.int32)
    outer = (core == right).astype(jnp.int32)
    return position, core, right, outer


def load(pairs, sems):
    copies = [pltpu.make_async_copy(src, dst, sems.at[k]) for k, (src, dst) in enumerate(pairs)]
    for copy in copies:
        copy.start()
    return copies


def prepared(ham, cpl):
    n = ham.shape[-1]
    _, core, _, _ = place()
    energy_count = lax.axis_size("energy")
    rank = lax.axis_index("energy")
    near = rank + 1 - 2 * (rank % 2)
    solved = jnp.where(core == 0, near, (rank + energy_count // 2) % energy_count)
    energy = -2.0 + (solved.astype(F32) + 0.5) * (4.0 / energy_count)
    one = unit(n)
    shift = energy * one + BROADENING * jnp.concatenate([one[:, n:], one[:, :n]], 1)
    hams = [row_form(ham, k) for k in range(2)]
    links = [row_form(cpl, k) for k in range(2)]
    return [shift - 0.5 * (m + adj(m)) for m in hams], links, [adj(m) for m in links]


BACK, CONTACT, LINKS = 4, 8, 10


def block_index(k):
    _, _, right, outer = place()
    return (2 * (1 - outer) if k < 2 else 2 * outer) + (k % 2 + right * (1 - 2 * (k % 2)))


def chip_index(j, core):
    return (2 * core if j < 2 else 2 * (1 - core)) + j % 2


def link_index(k):
    _, core, right, _ = place()
    at = jnp.where(right == 1, chip_index(2 - k, core), chip_index(k, core))
    return at + BACK * right, at + BACK * (1 - right)


def fill(ham, cpl, base, blocks_ref, links_ref):
    blocks, links, backs = prepared(ham, cpl)
    for k in range(2):
        blocks_ref[base + k] = blocks[k]
        links_ref[base + k] = links[k]
        links_ref[BACK + base + k] = backs[k]


def own_kernel(ham_hbm, cpl_hbm, contact_hbm, blocks_ref, links_ref, ham, cpl, contact, sems):
    for copy in load([(ham_hbm, ham), (cpl_hbm, cpl), (contact_hbm, contact)], sems):
        copy.wait()
    fill(ham, cpl, 0, blocks_ref, links_ref)
    lead = row_form(contact)
    links_ref[CONTACT] = lead
    links_ref[CONTACT + 1] = adj(lead)


def join_kernel(own_blocks, own_links, ham, cpl, blocks_ref, links_ref, head_ref):
    _, core, right, _ = place()
    fill(ham, cpl, 2, blocks_ref, links_ref)
    end = chip_index(3, core)
    lead = links_ref[jnp.where(right == 1, BACK + end, CONTACT)]
    lead_back = links_ref[jnp.where(right == 1, end, CONTACT + 1)]
    head_ref[...] = times_half_imag(mul(lead, lead_back))


B0, B1, B2, T0, P1, P2, Q, R, RECORD = range(9)


def chain_links(turned):
    found = [link_index(k) for k in range(3)]
    if turned:
        found = [(b, a) for a, b in found[::-1]]
    return [a for a, _ in found] + [b for _, b in found]


def eliminate(blocks, links, head, record, schur_ref, corner_ref, invert):
    c0, c1, c2, c0h, c1h, c2h = links
    (b0, b2), bad = invert([blocks[0] + head, blocks[2]])
    t0 = mul(b0, c0)
    p1 = mul(b2, c1h)
    p2 = mul(b2, c2)
    record[B0], record[B2], record[T0], record[P1], record[P2] = b0, b2, t0, p1, p2
    behind = mul(jnp.concatenate([c1, c2h], 0), p1)
    middle = blocks[1] - mul(c0h, t0) - behind[: c1.shape[0]]
    lower = behind[c1.shape[0] :]
    ahead = mul(jnp.concatenate([c1, c2h], 0), p2)
    upper = ahead[: c1.shape[0]]
    tail = blocks[3] - ahead[c1.shape[0] :]
    (b1,), more = invert([middle])
    bad = jnp.maximum(bad, more)
    q = mul(b1, upper)
    r = mul(lower, b1)
    schur = tail - mul(lower, q)
    record[B1], record[Q], record[R] = b1, q, r
    schur_ref[...] = schur
    (corner,), more = invert([schur])
    corner_ref[...] = corner
    return jnp.maximum(bad, more)


def send(links_ref, corner_ref, sender):
    _, core, right, _ = place()
    end = chip_index(3, core)

    @pl.when(right == sender)
    def _():
        corner_ref[...] = mul_split(mul_split(links_ref[BACK + end], corner_ref[...]), links_ref[end])


def receive(links_ref, message_ref, sigma_ref, multiplies):
    _, core, right, _ = place()
    end = chip_index(3, core)

    @pl.when(right == multiplies)
    def _():
        sigma_ref[...] = mul_split(mul_split(links_ref[end], message_ref[...]), links_ref[BACK + end])

    @pl.when(right != multiplies)
    def _():
        sigma_ref[...] = message_ref[...]


def head_kernel(multiplies, links_ref, message_ref, out_ref):
    receive(links_ref, message_ref, out_ref, multiplies)
    out_ref[...] = -out_ref[...]


def eliminate_kernel(turned, blocks_ref, links_ref, head_ref, record_ref, schur_ref, corner_ref):
    def run(invert):
        bad = eliminate(
            [blocks_ref[block_index(3 - k if turned else k)] for k in range(4)],
            [links_ref[at] for at in chain_links(turned)],
            head_ref[...],
            record_ref,
            schur_ref,
            corner_ref,
            invert,
        )
        send(links_ref, corner_ref, 1 if turned else 0)
        return bad

    bad = jnp.sum(run(invert_fast))

    @pl.when(jnp.logical_not(bad < RESIDUE_LIMIT))
    def _():
        run(invert_safe)


def spread_kernel(weight_ref, offset_ref, links_ref, record_ref, out_ref, weights_ref):
    for k, value in enumerate(weights(weight_ref, offset_ref)):
        weights_ref[k] = jnp.full(weights_ref.shape[1:], value, F32)
    _, c1, _, c0h, _, c2h = (links_ref[at] for at in chain_links(False))
    b0, b1, b2, t0, p1, p2, q, r = (record_ref[k] for k in range(RECORD))
    w0 = mul(c0h, b0)
    m1 = mul(c1, b2)
    m2 = mul(c2h, b2)
    out_ref[0] = b0 + mul(mul(t0, b1), w0)
    out_ref[1] = b1
    out_ref[2] = b2 + mul(mul(p1, b1), m1)
    out_ref[3] = mul(t0, q)
    out_ref[4] = q
    out_ref[5] = mul(p1, q) + p2
    out_ref[6] = mul(r, w0)
    out_ref[7] = r
    out_ref[8] = mul(r, m1) + m2


def finish_kernel(schur_ref, spread_ref, links_ref, message_ref, mine_ref, theirs_ref, sigma_ref):
    _, _, right, outer = place()
    n = schur_ref.shape[0]
    receive(links_ref, message_ref, sigma_ref, 0)

    def run(invert):
        closed = schur_ref[...] - sigma_ref[...]
        (full,), bad = invert([closed])
        reach = mul_split(jnp.concatenate([spread_ref[3 + j] for j in range(3)], 0), full)
        green = [spread_ref[j] + mul_split(reach[j * n : (j + 1) * n], spread_ref[6 + j]) for j in range(3)] + [full]

        def store(outer_ref, inner_ref):
            for k in range(4):
                ref = outer_ref if k < 2 else inner_ref
                index = jnp.where(right == 1, 1 - k % 2, k % 2)
                ref[index, 0] = green[k][:, :n]
                ref[index, 1] = green[k][:, n:]

        @pl.when(outer == 1)
        def _():
            store(mine_ref, theirs_ref)

        @pl.when(outer == 0)
        def _():
            store(theirs_ref, mine_ref)

        return bad

    bad = jnp.sum(run(invert_fast))

    @pl.when(jnp.logical_not(bad < RESIDUE_LIMIT))
    def _():
        run(invert_safe)


def weights(weight_ref, offset_ref):
    _, core, _, _ = place()
    energy_count = lax.axis_size("energy")
    rank = lax.axis_index("energy")
    near = rank + 1 - 2 * (rank % 2)

    def weight_of(source):
        found = jnp.float32(0.0)
        for m in range(weight_ref.shape[0]):
            found = found + jnp.where(offset_ref[m] == rank - source, weight_ref[m], 0.0)
        return found

    near_weight = weight_of(near)
    far_weight = weight_of((rank + energy_count // 2) % energy_count)
    mine = jnp.where(core == 0, near_weight, far_weight)
    partner = jnp.where(core == 0, far_weight, near_weight)
    return mine, partner, weight_of(2 * rank - near)


def combine_kernel(weights_ref, mine_ref, partner_ref, third_ref, pattern_ref, out_ref):
    mine, partner, away = (weights_ref[k, 0:1, :] for k in range(3))
    keep = pattern_ref[...].astype(F32)
    for k in range(out_ref.shape[1]):
        for part in range(2):
            value = mine * mine_ref[k, part] + partner * partner_ref[k, part]
            out_ref[0, k, part] = (value + away * third_ref[k, part]) * keep


def kernel(body, shapes, where, scratch=(), aliases=None, result="v"):
    spaces = {"s": pltpu.SMEM, "v": pltpu.VMEM, "a": pl.ANY, "h": pltpu.HBM}
    many = len(shapes) > 1
    if result == "v":
        outs = [pltpu.VMEM(shape, F32) for shape in shapes]
    else:
        outs = [jax.ShapeDtypeStruct(shape, F32) for shape in shapes]
    out_specs = [pl.BlockSpec(memory_space=pltpu.VMEM) for _ in shapes]
    call = pl.pallas_call(
        body,
        out_shape=outs if many else outs[0],
        in_specs=[pl.BlockSpec(memory_space=spaces[w]) for w in where],
        out_specs=out_specs if many else out_specs[0],
        scratch_shapes=list(scratch),
        input_output_aliases=aliases or {},
        compiler_params=pltpu.CompilerParams(vmem_limit_bytes=KERNEL_VMEM),
    )

    def placed(*operands):
        return call(*(
            pltpu.with_memory_space_constraint(x, spaces[w]) if w in "vh" else x for x, w in zip(operands, where)
        ))

    return placed


def on_device(ham_diag, coupling, contact_left, mode_weight, mode_offset, pattern):
    n = ham_diag.shape[-1]
    assert ham_diag.shape[0] == 2
    space = lax.axis_size("space")
    energies = lax.axis_size("energy")
    chips = space // 2
    middle = chips // 2
    assert chips % 2 == 0 and space % 2 == 0 and energies % 4 == 0
    position = lax.axis_index("space")
    chip = position // 2
    depth = jnp.where(chip < middle, chip, chips - 1 - chip)
    swap = [(p, p ^ 1) for p in range(space)]

    row = (n, 2 * n)
    pair = (2, 2, n, n)
    vmem = lambda *shape: pltpu.VMEM(shape, F32)
    sems = lambda count: pltpu.SemaphoreType.DMA((count,))

    ham_far = lax.ppermute(ham_diag, "space", swap)
    cpl_far = lax.ppermute(coupling, "space", swap)

    own = kernel(
        own_kernel, [(4,) + row, (LINKS,) + row], "hhh", [vmem(*pair), vmem(*pair), vmem(2, n, n), sems(3)]
    )(ham_diag, coupling, contact_left)
    blocks, links, head = kernel(
        join_kernel, [(4,) + row, (LINKS,) + row, row], "vvvv", aliases={0: 0, 1: 1}
    )(*own, ham_far, cpl_far)
    forward, backward = (
        kernel(functools.partial(eliminate_kernel, turned), [(RECORD,) + row, row, row], "vvv")
        for turned in (False, True)
    )

    def chip_move(value, pairs):
        return lax.ppermute(value, "space", [(2 * a + k, 2 * b + k) for a, b in pairs for k in range(2)])

    state = forward(blocks, links, head)

    head_inward, head_outward = (
        kernel(functools.partial(head_kernel, multiplies), [row], "vv") for multiplies in (1, 0)
    )
    for d in range(1, middle):
        inward = [(c, c + 1) for c in range(middle - 1)] + [(c + 1, c) for c in range(middle, chips - 1)]
        fresh = forward(blocks, links, head_inward(links, chip_move(state[2], inward)))
        state = [jnp.where(depth >= d, a, b) for a, b in zip(fresh, state)]
    record, schur, corner = state

    message = chip_move(corner, [(middle - 1, middle), (middle, middle - 1)])
    spread, shares = kernel(spread_kernel, [(9,) + row, (3, 8, n)], "ssvv")(
        mode_weight, mode_offset, links, record
    )
    for d in range(middle - 2, -1, -1):
        outward = [(c + 1, c) for c in range(middle - 1)] + [(c, c + 1) for c in range(middle, chips - 1)]
        fresh = backward(blocks, links, head_outward(links, message))
        message = jnp.where(depth == d, chip_move(fresh[2], outward), message)

    mine, theirs = kernel(finish_kernel, [pair, pair], "vvvv", [vmem(*row)])(
        schur, spread, links, message
    )
    ends_from = [(e + 1 - 2 * (1 - e % 2), e) for e in range(energies)]
    wanted = [(source, e) for source, e in ends_from if 0 <= source < energies]
    pairs = []
    for c in range(chips):
        for source, e in wanted:
            for k, site in enumerate((source + 1 - 2 * (source % 2), (source + energies // 2) % energies)):
                pairs.append(((2 * c + k) * energies + site, (2 * c + k) * energies + e))
    third = lax.ppermute(mine, ("space", "energy"), pairs)
    partner = lax.ppermute(theirs, "space", swap)
    return kernel(combine_kernel, [(1,) + pair], "vvvvv", result="a")(shares, mine, partner, third, pattern)


def solution(mesh):
    placed = (P("space", None, None, None), P("space", None, None, None), P(), P(), P(), P())
    return jax.shard_map(
        on_device,
        mesh=mesh,
        in_specs=placed,
        out_specs=P("energy", "space", None, None, None),
        check_vma=False,
    )
```
